256 devices in a mesh: tower: 4 (over x_lo, core), seq: 64 (over x_hi, z, y).
Axes of the slice: x: 4 (x_hi: 2, x_lo: 2; x = x_hi * 2 + x_lo), y: 4, z: 8, core: 2. Of those that a mesh axis runs over, the one named last changes fastest.
Arguments:
- queries: bfloat16 [4, 8192, 3072], P('tower', 'seq'), may hold values from -100 to 100
- keys: bfloat16 [4, 8192, 3072], P('tower', 'seq'), may hold values from -4 to 4
- values: bfloat16 [4, 8192, 3072], P('tower', 'seq'), may hold values from -6 to 6
- alignment: int32 [64, 2], replicated, may hold values from 0 to 192, as said below
- cross_gate: float32 [2, 24], replicated, may hold values from 0.5 to 2
Outputs:
- cross_out: bfloat16 [4, 8192, 3072], P('tower', 'seq')
The draws below stay inside these ranges and needn't reach their ends.
Inputs may be any that keep to these rules, and one draw needn't show every extreme that they name: `alignment`: lo[a] is max(3a - 1, 0) or max(3a, 0); hi[a] is min(3a + 3, 192) or min(3a + 4, 192).
All inputs are finite; a program needn't handle non-finite values.
Results may differ from the reference program's by a relative error of at most 0.0044.
Values may be sent and summed in bfloat16 or wider, within the bound.
A program may use at most 128 MiB of HBM per device.

```python
import math
import jax
import jax.numpy as jnp
from jax import lax

D = 3072
HEADS = 24
HEAD_DIM = 128
BLOCK = 128
TOK_DEV = 128
ROWS = 8192
NV = 192
NA = 64
N_SEQ = 64


def key_field(key):
    return jnp.clip(jax.random.normal(jax.random.fold_in(key, 7), (4, ROWS, D), jnp.float32), -4.0, 4.0)


def draw_keys(key, part):
    return key_field(key).astype(jnp.bfloat16)


def draw_queries(key, part):
    base = jax.random.normal(jax.random.fold_in(key, 8), (4, ROWS, D), jnp.float32)
    return base.astype(jnp.bfloat16)


def draw_alignment(key, part):
    index = jnp.arange(NA, dtype=jnp.int32)
    early = jax.random.randint(jax.random.fold_in(key, 21), (NA,), 0, 2, jnp.int32)
    late = jax.random.randint(jax.random.fold_in(key, 22), (NA,), 0, 2, jnp.int32)
    lows = jnp.maximum(3 * index - early, 0)
    highs = jnp.minimum(3 * index + 3 + late, NV)
    return jnp.stack([lows, highs], axis=1).astype(jnp.int32)


def level_of(rng, dims, shards, low, top_value):
    def one(axis_at, blocks):
        steps = jax.random.uniform(jax.random.fold_in(jax.random.fold_in(rng, 6), axis_at), (blocks,), jnp.float32, low / len(shards), top_value / len(shards))
        return jnp.repeat(jnp.exp(steps), dims[axis_at] // blocks).reshape((-1,) + (1,) * (len(dims) - axis_at - 1))

    level = one(*shards[0])
    for cut in shards[1:]:
        level = level * one(*cut)
    return level


def centred(own_key, dims, deviation, limit, cuts=(), held_as=jnp.bfloat16):
    level = level_of(own_key, dims, cuts, -0.22, 0.18) if cuts else 1.0
    result = jax.random.normal(own_key, dims, jnp.float32) * deviation * level
    return jnp.minimum(jnp.maximum(result, -limit), limit).astype(held_as)


def setup_inputs(seed: int = 0) -> dict:
    splits = jax.random.split(jax.random.key(seed), 6)
    return {
        "queries": draw_queries(jax.random.fold_in(splits[5], 71), 0),
        "keys": draw_keys(jax.random.fold_in(splits[5], 71), 0),
        "values": centred(splits[2], (4, ROWS, D), 1.0, 6.0, ((0, 4), (1, 64))),
        "alignment": draw_alignment(jax.random.fold_in(splits[5], 71), 0),
        "cross_gate": jnp.clip(jnp.exp(jax.random.uniform(splits[4], (2, HEADS), jnp.float32, math.log(0.5), math.log(2.0))), 0.5, 2.0),
    }


def attend(query_block, key_rows, value_rows, valid, gain):
    count_q = query_block.shape[0]
    count_k = key_rows.shape[0]
    q_heads = query_block.astype(jnp.float32).reshape(count_q, HEADS, HEAD_DIM)
    k_heads = key_rows.astype(jnp.float32).reshape(count_k, HEADS, HEAD_DIM)
    v_heads = value_rows.astype(jnp.float32).reshape(count_k, HEADS, HEAD_DIM)
    scores = jnp.einsum("qhd,khd->hqk", q_heads, k_heads) * (HEAD_DIM ** -0.5)
    scores = jnp.where(valid[None, None, :], scores, -jnp.inf)
    top = jnp.max(scores, axis=2, keepdims=True)
    weights = jnp.exp(scores - top)
    total = jnp.sum(weights, axis=2)
    rounded = lax.optimization_barrier(weights.astype(jnp.bfloat16)).astype(jnp.float32)
    mixed = jnp.einsum("hqk,khd->qhd", rounded, v_heads)
    mixed = mixed / jnp.transpose(total)[:, :, None] * gain[None, :, None]
    return mixed.reshape(count_q, HEADS * HEAD_DIM)


def reference(queries, keys, values, alignment, cross_gate):
    per_dev = TOK_DEV // BLOCK
    lows = alignment[:, 0]
    highs = alignment[:, 1]

    def video_order(field):
        split = field[:3].reshape(3, N_SEQ, per_dev, BLOCK, D)
        return jnp.transpose(split, (1, 0, 2, 3, 4)).reshape(NV, BLOCK, D)

    def padded(blocks):
        return jnp.pad(blocks, ((1, 1), (0, 0), (0, 0)))

    audio_keys = padded(keys[3].reshape(NA, BLOCK, D))
    audio_values = padded(values[3].reshape(NA, BLOCK, D))
    video_keys = padded(video_order(keys))
    video_values = padded(video_order(values))

    def video_step(item):
        index, query_block = item
        first = index // 3 - 1
        key_rows = lax.dynamic_slice_in_dim(audio_keys, first + 1, 3, 0).reshape(3 * BLOCK, D)
        value_rows = lax.dynamic_slice_in_dim(audio_values, first + 1, 3, 0).reshape(3 * BLOCK, D)
        near = first + jnp.arange(3, dtype=jnp.int32)
        safe = jnp.clip(near, 0, NA - 1)
        linked = (near >= 0) & (near < NA) & (lows[safe] <= index) & (index < highs[safe])
        return attend(query_block, key_rows, value_rows, jnp.repeat(linked, BLOCK), cross_gate[0])

    def audio_step(item):
        index, query_block = item
        first = 3 * index - 1
        key_rows = lax.dynamic_slice_in_dim(video_keys, first + 1, 5, 0).reshape(5 * BLOCK, D)
        value_rows = lax.dynamic_slice_in_dim(video_values, first + 1, 5, 0).reshape(5 * BLOCK, D)
        near = first + jnp.arange(5, dtype=jnp.int32)
        linked = (near >= 0) & (near < NV) & (lows[index] <= near) & (near < highs[index])
        return attend(query_block, key_rows, value_rows, jnp.repeat(linked, BLOCK), cross_gate[1])

    video_out = lax.map(video_step, (jnp.arange(NV, dtype=jnp.int32), video_order(queries)))
    audio_out = lax.map(audio_step, (jnp.arange(NA, dtype=jnp.int32), queries[3].reshape(NA, BLOCK, D)))
    video_back = jnp.transpose(video_out.reshape(N_SEQ, 3, per_dev, BLOCK, D), (1, 0, 2, 3, 4)).reshape(3, ROWS, D)
    whole = jnp.concatenate([video_back, audio_out.reshape(1, ROWS, D)], axis=0)
    return whole.astype(jnp.bfloat16)
```

```python
import functools
import math

import jax
import jax.numpy as jnp
from jax import lax
from jax.experimental import pallas as pl
from jax.experimental.pallas import tpu as pltpu
from jax.sharding import PartitionSpec as P

HEADS = 24
DIM = 128
BLOCK = 128
WIDTH = HEADS * DIM
PER = 2
CHUNKS = HEADS // PER
HALF = CHUNKS // 2
SPAN = PER * DIM
COLD = math.log2(math.e) / math.sqrt(DIM)
MESH = pl.DeviceIdType.MESH


def cols(chunk):
    return pl.ds(pl.multiple_of(chunk * SPAN, SPAN), SPAN)


def head_cols(head):
    return pl.ds(pl.multiple_of(head * DIM, DIM), DIM)


def loop(count, body):
    def step(i, carry):
        body(i)
        return carry

    lax.fori_loop(0, count, step, 0)


def mix(q, k, v, bias):
    scores = lax.dot_general(q, k, (((1,), (1,)), ((), ())), preferred_element_type=jnp.float32)
    if bias is not None:
        scores = scores + bias
    top = jnp.max(scores, axis=1, keepdims=True)
    weights = jnp.exp2((scores - top) * COLD)
    total = jnp.sum(weights, axis=1, keepdims=True)
    mixed = jnp.dot(weights.astype(jnp.bfloat16), v, preferred_element_type=jnp.float32)
    return mixed, top, total


def bias_row(linked, blocks):
    off = jnp.where(linked, 0.0, -jnp.inf).astype(jnp.float32)
    place = lax.broadcasted_iota(jnp.int32, (1, blocks * BLOCK), 1)
    return jnp.where(place >= (blocks - 1) * BLOCK, off, 0.0)


def kernel(
    seq_count,
    align_ref,
    gate_ref,
    q_hbm,
    k_hbm,
    v_hbm,
    out_hbm,
    q_own,
    main_k,
    main_v,
    aud_q,
    aud_k,
    aud_v,
    part_out,
    part_stat,
    part_in,
    stat_in,
    local_mix,
    local_top,
    local_total,
    out_buf,
    local_sem,
    out_sem,
    send_a,
    send_b,
    send_c,
    send_d,
    recv_near,
    recv_next,
    recv_q,
    recv_pair,
    recv_third,
    recv_part,
    recv_stat,
):
    tower = lax.axis_index("tower")
    column = lax.axis_index("seq")
    is_first = column == 0
    is_last = column == seq_count - 1
    before = jnp.maximum(column - 1, 0)
    after = jnp.minimum(column + 1, seq_count - 1)
    sources = (k_hbm, v_hbm)
    mains = (main_k, main_v)
    auds = (aud_k, aud_v)

    def device(t, c):
        return {"tower": t, "seq": c}

    def remote(src, dst, send, recv, t, c):
        return pltpu.make_async_remote_copy(
            src_ref=src, dst_ref=dst, send_sem=send, recv_sem=recv, device_id=device(t, c), device_id_type=MESH
        )

    q_copy = pltpu.make_async_copy(q_hbm.at[0], q_own, local_sem.at[2])
    q_copy.start()

    barrier = pltpu.get_barrier_semaphore()

    def greet(t, c):
        pl.semaphore_signal(barrier, inc=1, device_id=device(t, c), device_id_type=MESH)

    def meet(fixed, backward, forward):
        for t in fixed:
            greet(t, column)

        @pl.when(jnp.logical_not(is_first))
        def _():
            for t in backward:
                greet(t, before)

        @pl.when(jnp.logical_not(is_last))
        def _():
            for t in forward:
                greet(t, after)

        peers = jnp.int32(len(fixed))
        peers = peers + jnp.where(is_first, 0, len(backward))
        peers = peers + jnp.where(is_last, 0, len(forward))
        pl.semaphore_wait(barrier, peers)

    @pl.when(tower == 0)
    def _():
        meet((1, 3), (0, 1), (0,))

    @pl.when(tower == 1)
    def _():
        meet((0, 3), (), (0,))

    @pl.when(tower == 2)
    def _():
        meet((3,), (), (3,))

    @pl.when(tower == 3)
    def _():
        meet((0, 1, 2), (2,), ())

    near_rows = pl.ds(0, BLOCK)
    next_rows = pl.ds(BLOCK, BLOCK)
    third_rows = pl.ds(2 * BLOCK, BLOCK)

    def write_out(chunk):
        return pltpu.make_async_copy(
            out_buf.at[:, cols(chunk)], out_hbm.at[0, :, cols(chunk)], out_sem.at[chunk]
        )

    def recv_main(which, chunk, rows, sems):
        dst = mains[which].at[rows, cols(chunk)]
        return remote(dst, dst, send_a.at[which, chunk], sems.at[which, chunk], tower, column)

    def await_near(chunk):
        for which in range(2):
            recv_main(which, chunk, near_rows, recv_near).wait_recv()

    def await_next(chunk):
        for which in range(2):
            recv_main(which, chunk, next_rows, recv_next).wait_recv()

    def video_heads(chunk, blocks, bias):
        for i in range(PER):
            head = chunk * PER + i
            at = head_cols(head)
            mixed, _, total = mix(
                q_own[:, at], main_k[0 : blocks * BLOCK, at], main_v[0 : blocks * BLOCK, at], bias
            )
            out_buf[:, at] = (mixed * (gate_ref[0, head] / total)).astype(jnp.bfloat16)
        write_out(chunk).start()

    def finish_out(chunk):
        write_out(chunk).wait()

    @pl.when(tower < 2)
    def _():
        other = 1 - tower
        own_base = tower * HALF
        other_base = other * HALF
        own_rows = pl.ds(pl.multiple_of(tower * BLOCK, BLOCK), BLOCK)
        half_cols = pl.ds(pl.multiple_of(own_base * SPAN, SPAN), HALF * SPAN)
        other_cols = pl.ds(pl.multiple_of(other_base * SPAN, SPAN), HALF * SPAN)
        pair_rows = pl.ds(pl.multiple_of(other * BLOCK, BLOCK), BLOCK)

        def own_copy(which):
            return pltpu.make_async_copy(
                sources[which].at[0, :, half_cols], auds[which].at[own_rows, :], local_sem.at[which]
            )

        def pair_copy(which):
            return remote(
                sources[which].at[0, :, other_cols],
                auds[which].at[own_rows, :],
                send_c.at[which, 0],
                recv_pair.at[which],
                other,
                column,
            )

        def pair_wait(which):
            dst = auds[which].at[pair_rows, :]
            return remote(dst, dst, send_c.at[which, 0], recv_pair.at[which], tower, column)

        def third_copy(which, half, chunk):
            src = sources[which].at[0, :, cols(half * HALF + chunk)]
            dst = auds[which].at[third_rows, cols(chunk)]
            return remote(
                src, dst, send_d.at[which, half * HALF + chunk], recv_third.at[which, chunk], half, before
            )

        def third_wait(which, chunk):
            dst = auds[which].at[third_rows, cols(chunk)]
            return remote(dst, dst, send_d.at[which, chunk], recv_third.at[which, chunk], tower, column)

        def pass_pair(which, chunk):
            part = mains[which].at[near_rows, cols(chunk)]
            return remote(part, part, send_a.at[which, chunk], recv_near.at[which, chunk], other, column)

        def pass_next(which, chunk):
            return remote(
                mains[which].at[near_rows, cols(chunk)],
                mains[which].at[next_rows, cols(chunk)],
                send_b.at[which, chunk],
                recv_next.at[which, chunk],
                0,
                after,
            )

        def part_copy(chunk):
            return remote(
                part_out.at[:, cols(chunk)],
                part_in.at[:, cols(own_base + chunk)],
                send_c.at[0, 1 + chunk],
                recv_part.at[own_base + chunk],
                3,
                column,
            )

        def stat_copy(chunk):
            return remote(
                part_stat.at[chunk],
                stat_in.at[own_base + chunk],
                send_c.at[1, 1 + chunk],
                recv_stat.at[own_base + chunk],
                3,
                column,
            )

        for which in range(2):
            pair_copy(which).start()

        @pl.when(jnp.logical_and(tower == 0, jnp.logical_not(is_first)))
        def _():
            def start(chunk):
                for half in range(2):
                    for which in range(2):
                        third_copy(which, half, chunk).start()

            loop(HALF, start)

        for which in range(2):
            own_copy(which).start()

        @pl.when(jnp.logical_and(tower == 0, is_first))
        def _():
            for ref in mains:
                ref[BLOCK : 2 * BLOCK, :] = jnp.zeros((BLOCK, WIDTH), jnp.bfloat16)

        @pl.when(is_last)
        def _():
            for ref in auds:
                ref[2 * BLOCK : 3 * BLOCK, :] = jnp.zeros((BLOCK, WIDTH // 2), jnp.bfloat16)

        q_copy.wait()
        video_bias = bias_row(jnp.logical_and(column > 0, align_ref[before, 1] > 3 * column), 2)
        audio_bias = bias_row(align_ref[column, 1] > 3 * column + 3, 3)

        def video(step):
            @pl.when(tower == 0)
            def _():
                for base in (0, HALF):
                    chunk = base + step

                    @pl.when(jnp.logical_not(is_first))
                    def _():
                        await_next(chunk)

            await_near(other_base + step)

            @pl.when(tower == 0)
            def _():
                for base in (0, HALF):
                    video_heads(base + step, 2, video_bias)

            @pl.when(tower == 1)
            def _():
                for base in (0, HALF):
                    video_heads(base + step, 1, None)

        def take(step):
            chunk = own_base + step
            await_near(chunk)
            for which in range(2):
                pass_pair(which, chunk).start()

            @pl.when(jnp.logical_not(is_last))
            def _():
                for which in range(2):
                    pass_next(which, chunk).start()

            @pl.when(step > 0)
            def _():
                video(step - 1)

        loop(HALF, take)
        video(HALF - 1)

        for which in range(2):
            own_copy(which).wait()
            pair_wait(which).wait_recv()

        def audio(step):
            dst = aud_q.at[:, cols(step)]
            remote(dst, dst, send_a.at[0, step], recv_q.at[step], tower, column).wait_recv()

            @pl.when(jnp.logical_not(is_last))
            def _():
                for which in range(2):
                    third_wait(which, step).wait_recv()

            lane = lax.broadcasted_iota(jnp.int32, (BLOCK, DIM), 1)
            stat = jnp.zeros((BLOCK, DIM), jnp.float32)
            for i in range(PER):
                at = head_cols(step * PER + i)
                mixed, top, total = mix(aud_q[:, at], aud_k[:, at], aud_v[:, at], audio_bias)
                part_out[:, at] = mixed.astype(jnp.bfloat16)
                stat = jnp.where(lane == 2 * i, top, stat)
                stat = jnp.where(lane == 2 * i + 1, total, stat)
            part_stat[step] = jnp.transpose(stat)[0:8]
            stat_copy(step).start()
            part_copy(step).start()

        loop(HALF, audio)

        for which in range(2):
            pair_copy(which).wait_send()

        @pl.when(jnp.logical_and(tower == 0, jnp.logical_not(is_first)))
        def _():
            def drain(chunk):
                for half in range(2):
                    for which in range(2):
                        third_copy(which, half, chunk).wait_send()

            loop(HALF, drain)

        def drain(step):
            chunk = own_base + step
            for which in range(2):
                pass_pair(which, chunk).wait_send()

            @pl.when(jnp.logical_not(is_last))
            def _():
                for which in range(2):
                    pass_next(which, chunk).wait_send()

            stat_copy(step).wait_send()
            part_copy(step).wait_send()

        loop(HALF, drain)
        loop(CHUNKS, finish_out)

    @pl.when(tower == 2)
    def _():
        def near_copy(which, chunk):
            return remote(
                sources[which].at[0, :, cols(chunk)],
                mains[which].at[near_rows, cols(chunk)],
                send_a.at[which, chunk],
                recv_near.at[which, chunk],
                3,
                column,
            )

        def next_copy(which, chunk):
            return remote(
                sources[which].at[0, :, cols(chunk)],
                mains[which].at[next_rows, cols(chunk)],
                send_b.at[which, chunk],
                recv_next.at[which, chunk],
                3,
                after,
            )

        def start_near(chunk):
            for which in range(2):
                near_copy(which, chunk).start()

        def start_next(chunk):
            for which in range(2):
                next_copy(which, chunk).start()

        @pl.when(jnp.logical_not(is_last))
        def _():
            loop(CHUNKS, start_next)

        loop(CHUNKS, start_near)

        @pl.when(is_last)
        def _():
            for ref in mains:
                ref[BLOCK : 2 * BLOCK, :] = jnp.zeros((BLOCK, WIDTH), jnp.bfloat16)

        q_copy.wait()
        linked = jnp.logical_and(column < seq_count - 1, align_ref[after, 0] <= 3 * column + 2)
        bias = bias_row(linked, 2)

        def video(chunk):
            await_near(chunk)

            @pl.when(jnp.logical_not(is_last))
            def _():
                await_next(chunk)

            video_heads(chunk, 2, bias)

        loop(CHUNKS, video)

        def drain(chunk):
            for which in range(2):
                near_copy(which, chunk).wait_send()

            @pl.when(jnp.logical_not(is_last))
            def _():
                for which in range(2):
                    next_copy(which, chunk).wait_send()

            finish_out(chunk)

        loop(CHUNKS, drain)

    @pl.when(tower == 3)
    def _():
        def far_copy(which, half, step):
            chunk = half * HALF + step
            return remote(
                sources[which].at[0, :, cols(chunk)],
                mains[which].at[near_rows, cols(chunk)],
                send_a.at[which, chunk],
                recv_near.at[which, chunk],
                half,
                column,
            )

        def query_copy(half, step):
            return remote(
                q_hbm.at[0, :, cols(half * HALF + step)],
                aud_q.at[:, cols(step)],
                send_d.at[half, step],
                recv_q.at[step],
                half,
                column,
            )

        def near_copy(which, chunk):
            return remote(
                sources[which].at[0, :, cols(chunk)],
                mains[which].at[near_rows, cols(chunk)],
                send_b.at[which, chunk],
                recv_near.at[which, chunk],
                2,
                column,
            )

        def back_copy(which, chunk):
            return remote(
                sources[which].at[0, :, cols(chunk)],
                mains[which].at[next_rows, cols(chunk)],
                send_c.at[which, chunk],
                recv_next.at[which, chunk],
                2,
                before,
            )

        def start_far(step):
            for half in range(2):
                for which in range(2):
                    far_copy(which, half, step).start()

        loop(HALF, start_far)

        def start_query(step):
            for half in range(2):
                query_copy(half, step).start()

        loop(HALF, start_query)

        @pl.when(jnp.logical_not(is_first))
        def _():
            def start_back(chunk):
                for which in range(2):
                    back_copy(which, chunk).start()

            loop(CHUNKS, start_back)

        def start_near(chunk):
            for which in range(2):
                near_copy(which, chunk).start()

        loop(CHUNKS, start_near)

        @pl.when(is_first)
        def _():
            for ref in mains:
                ref[BLOCK : 2 * BLOCK, :] = jnp.zeros((BLOCK, WIDTH), jnp.bfloat16)

        q_copy.wait()
        bias = bias_row(align_ref[column, 0] <= 3 * column - 1, 2)

        def local(chunk):
            await_near(chunk)

            @pl.when(jnp.logical_not(is_first))
            def _():
                await_next(chunk)

            for i in range(PER):
                head = chunk * PER + i
                at = head_cols(head)
                mixed, top, total = mix(q_own[:, at], main_k[:, at], main_v[:, at], bias)
                local_mix[:, at] = mixed
                local_top[head] = jnp.broadcast_to(top, (BLOCK, DIM))
                local_total[head] = jnp.broadcast_to(total, (BLOCK, DIM))

        loop(CHUNKS, local)

        def merge_chunk(chunk):
            dst = stat_in.at[chunk]
            remote(dst, dst, send_a.at[0, chunk], recv_stat.at[chunk], tower, column).wait_recv()
            dst = part_in.at[:, cols(chunk)]
            remote(dst, dst, send_a.at[0, chunk], recv_part.at[chunk], tower, column).wait_recv()
            stat = jnp.concatenate([stat_in[chunk], jnp.zeros((DIM - 8, BLOCK), jnp.float32)], axis=0)
            stat = jnp.transpose(stat)
            for i in range(PER):
                head = chunk * PER + i
                at = head_cols(head)
                far_top = stat[:, 2 * i : 2 * i + 1]
                far_total = stat[:, 2 * i + 1 : 2 * i + 2]
                near_top = local_top[head][:, 0:1]
                near_total = local_total[head][:, 0:1]
                top = jnp.maximum(far_top, near_top)
                far = jnp.exp2((far_top - top) * COLD)
                near = jnp.exp2((near_top - top) * COLD)
                scale = gate_ref[1, head] / (far * far_total + near * near_total)
                mixed = part_in[:, at].astype(jnp.float32) * (far * scale) + local_mix[:, at] * (near * scale)
                out_buf[:, at] = mixed.astype(jnp.bfloat16)
            write_out(chunk).start()

        def merge(step):
            for half in range(2):
                merge_chunk(half * HALF + step)

        loop(HALF, merge)

        def drain_far(step):
            for half in range(2):
                for which in range(2):
                    far_copy(which, half, step).wait_send()
                query_copy(half, step).wait_send()

        loop(HALF, drain_far)

        def drain(chunk):
            for which in range(2):
                near_copy(which, chunk).wait_send()

            @pl.when(jnp.logical_not(is_first))
            def _():
                for which in range(2):
                    back_copy(which, chunk).wait_send()

            finish_out(chunk)

        loop(CHUNKS, drain)


def local(seq_count, queries, keys, values, alignment, cross_gate):
    bf16, f32 = jnp.bfloat16, jnp.float32
    dma = pltpu.SemaphoreType.DMA
    any_space = pl.BlockSpec(memory_space=pl.ANY)
    smem = pl.BlockSpec(memory_space=pltpu.SMEM)
    return pl.pallas_call(
        functools.partial(kernel, seq_count),
        out_shape=jax.ShapeDtypeStruct(queries.shape, bf16),
        in_specs=[smem, smem, any_space, any_space, any_space],
        out_specs=any_space,
        scratch_shapes=[
            pltpu.VMEM((BLOCK, WIDTH), bf16),
            pltpu.VMEM((2 * BLOCK, WIDTH), bf16),
            pltpu.VMEM((2 * BLOCK, WIDTH), bf16),
            pltpu.VMEM((BLOCK, WIDTH // 2), bf16),
            pltpu.VMEM((3 * BLOCK, WIDTH // 2), bf16),
            pltpu.VMEM((3 * BLOCK, WIDTH // 2), bf16),
            pltpu.VMEM((BLOCK, WIDTH // 2), bf16),
            pltpu.VMEM((HALF, 8, BLOCK), f32),
            pltpu.VMEM((BLOCK, WIDTH), bf16),
            pltpu.VMEM((CHUNKS, 8, BLOCK), f32),
            pltpu.VMEM((BLOCK, WIDTH), f32),
            pltpu.VMEM((HEADS, BLOCK, DIM), f32),
            pltpu.VMEM((HEADS, BLOCK, DIM), f32),
            pltpu.VMEM((BLOCK, WIDTH), bf16),
            dma((3,)),
            dma((CHUNKS,)),
            dma((2, CHUNKS)),
            dma((2, CHUNKS)),
            dma((2, CHUNKS)),
            dma((2, CHUNKS)),
            dma((2, CHUNKS)),
            dma((2, CHUNKS)),
            dma((HALF,)),
            dma((2,)),
            dma((2, HALF)),
            dma((CHUNKS,)),
            dma((CHUNKS,)),
        ],
        compiler_params=pltpu.CompilerParams(
            collective_id=0, has_side_effects=True, vmem_limit_bytes=48 * 1024 * 1024
        ),
    )(alignment, cross_gate, queries, keys, values)


def solution(mesh):
    placed = (P("tower", "seq", None), P("tower", "seq", None), P("tower", "seq", None), P(), P())
    return jax.shard_map(
        functools.partial(local, mesh.shape["seq"]),
        mesh=mesh,
        in_specs=placed,
        out_specs=P("tower", "seq", None),
        check_vma=False,
    )
```

```python
import functools
import math

import jax
import jax.numpy as jnp
from jax import lax
from jax.experimental import pallas as pl
from jax.experimental.pallas import tpu as pltpu
from jax.sharding import PartitionSpec as P

HEADS = 24
DIM = 128
BLOCK = 128
WIDTH = HEADS * DIM
PER = 2
CHUNKS = HEADS // PER
HALF = CHUNKS // 2
SPAN = PER * DIM
COLD = math.log2(math.e) / math.sqrt(DIM)
MESH = pl.DeviceIdType.MESH


def cols(chunk):
    return pl.ds(pl.multiple_of(chunk * SPAN, SPAN), SPAN)


def head_cols(head):
    return pl.ds(pl.multiple_of(head * DIM, DIM), DIM)


def loop(count, body):
    def step(i, carry):
        body(i)
        return carry

    lax.fori_loop(0, count, step, 0)


def mix(q, k, v, bias):
    scores = lax.dot_general(q, k, (((1,), (1,)), ((), ())), preferred_element_type=jnp.float32)
    if bias is not None:
        scores = scores + bias
    top = jnp.max(scores, axis=1, keepdims=True)
    weights = jnp.exp2((scores - top) * COLD)
    total = jnp.sum(weights, axis=1, keepdims=True)
    mixed = jnp.dot(weights.astype(jnp.bfloat16), v, preferred_element_type=jnp.float32)
    return mixed, top, total


def bias_row(linked, blocks):
    off = jnp.where(linked, 0.0, -jnp.inf).astype(jnp.float32)
    place = lax.broadcasted_iota(jnp.int32, (1, blocks * BLOCK), 1)
    return jnp.where(place >= (blocks - 1) * BLOCK, off, 0.0)


def kernel(
    seq_count,
    align_hbm,
    gate_hbm,
    q_hbm,
    k_hbm,
    v_hbm,
    out_hbm,
    q_own,
    main_k,
    main_v,
    aud_q,
    aud_k,
    aud_v,
    part_out,
    part_stat,
    part_in,
    stat_in,
    local_mix,
    local_top,
    local_total,
    out_buf,
    align_ref,
    gate_ref,
    edge_k,
    edge_v,
    edge_q,
    edge_out,
    edge_stat,
    edge_in,
    edge_stat_in,
    relay_k,
    relay_v,
    local_sem,
    out_sem,
    send_a,
    send_b,
    send_c,
    send_d,
    recv_near,
    recv_next,
    recv_q,
    recv_pair,
    recv_third,
    recv_part,
    recv_stat,
    send_e,
    recv_edge_q,
    recv_edge,
    recv_edge_stat,
    recv_relay,
):
    tower = lax.axis_index("tower")
    column = lax.axis_index("seq")
    is_first = column == 0
    is_last = column == seq_count - 1
    edge = seq_count // 2 - 1
    last = seq_count - 1
    at_edge = column == edge
    past_edge = column == edge + 1
    before = jnp.maximum(column - 1, 0)
    after = jnp.minimum(column + 1, seq_count - 1)
    sources = (k_hbm, v_hbm)
    mains = (main_k, main_v)
    auds = (aud_k, aud_v)

    def device(t, c):
        return {"tower": t, "seq": c}

    def remote(src, dst, send, recv, t, c):
        return pltpu.make_async_remote_copy(
            src_ref=src, dst_ref=dst, send_sem=send, recv_sem=recv, device_id=device(t, c), device_id_type=MESH
        )

    q_copy = pltpu.make_async_copy(q_hbm.at[0], q_own, local_sem.at[2])
    q_copy.start()
    small = (
        pltpu.make_async_copy(align_hbm, align_ref, local_sem.at[3]),
        pltpu.make_async_copy(gate_hbm, gate_ref, local_sem.at[4]),
    )
    for copy in small:
        copy.start()

    barrier = pltpu.get_barrier_semaphore()

    def greet(t, c):
        pl.semaphore_signal(barrier, inc=1, device_id=device(t, c), device_id_type=MESH)

    def meet(fixed, others):
        peers = jnp.int32(len(fixed))
        for t in fixed:
            greet(t, column)
        for when, t, c in others:

            @pl.when(when)
            def _():
                greet(t, c)

            peers = peers + jnp.where(when, 1, 0)
        pl.semaphore_wait(barrier, peers)

    has_back = jnp.logical_not(jnp.logical_or(is_first, past_edge))
    has_forward = jnp.logical_not(jnp.logical_or(is_last, at_edge))

    @pl.when(tower == 0)
    def _():
        meet(
            (1, 3),
            [
                (has_back, 0, before),
                (has_back, 1, before),
                (has_forward, 0, after),
                (past_edge, 2, edge),
                (past_edge, 3, edge),
                (is_last, 2, edge),
                (is_last, 3, edge + 1),
            ],
        )

    @pl.when(tower == 1)
    def _():
        meet((0, 3), [(has_forward, 0, after), (past_edge, 2, edge)])

    @pl.when(tower == 2)
    def _():
        meet((3,), [(has_forward, 3, after), (at_edge, 0, edge + 1), (at_edge, 1, edge + 1), (at_edge, 0, last)])

    @pl.when(tower == 3)
    def _():
        meet((0, 1, 2), [(has_back, 2, before), (at_edge, 0, edge + 1), (past_edge, 0, last)])

    near_rows = pl.ds(0, BLOCK)
    next_rows = pl.ds(BLOCK, BLOCK)
    third_rows = pl.ds(2 * BLOCK, BLOCK)

    def await_own():
        q_copy.wait()
        for copy in small:
            copy.wait()

    def write_out(chunk):
        return pltpu.make_async_copy(
            out_buf.at[:, cols(chunk)], out_hbm.at[0, :, cols(chunk)], out_sem.at[chunk]
        )

    def recv_main(which, chunk, rows, sems):
        dst = mains[which].at[rows, cols(chunk)]
        return remote(dst, dst, send_a.at[which, chunk], sems.at[which, chunk], tower, column)

    def await_near(chunk):
        for which in range(2):
            recv_main(which, chunk, near_rows, recv_near).wait_recv()

    def await_next(chunk):
        for which in range(2):
            recv_main(which, chunk, next_rows, recv_next).wait_recv()

    def video_heads(chunk, blocks, bias):
        for i in range(PER):
            head = chunk * PER + i
            at = head_cols(head)
            mixed, _, total = mix(
                q_own[:, at], main_k[0 : blocks * BLOCK, at], main_v[0 : blocks * BLOCK, at], bias
            )
            out_buf[:, at] = (mixed * (gate_ref[0, head] / total)).astype(jnp.bfloat16)
        write_out(chunk).start()

    def finish_out(chunk):
        write_out(chunk).wait()

    @pl.when(tower < 2)
    def _():
        other = 1 - tower
        own_base = tower * HALF
        other_base = other * HALF
        own_rows = pl.ds(pl.multiple_of(tower * BLOCK, BLOCK), BLOCK)
        half_cols = pl.ds(pl.multiple_of(own_base * SPAN, SPAN), HALF * SPAN)
        other_cols = pl.ds(pl.multiple_of(other_base * SPAN, SPAN), HALF * SPAN)
        pair_rows = pl.ds(pl.multiple_of(other * BLOCK, BLOCK), BLOCK)

        def own_copy(which):
            return pltpu.make_async_copy(
                sources[which].at[0, :, half_cols], auds[which].at[own_rows, :], local_sem.at[which]
            )

        def pair_copy(which):
            return remote(
                sources[which].at[0, :, other_cols],
                auds[which].at[own_rows, :],
                send_c.at[which, 0],
                recv_pair.at[which],
                other,
                column,
            )

        def pair_wait(which):
            dst = auds[which].at[pair_rows, :]
            return remote(dst, dst, send_c.at[which, 0], recv_pair.at[which], tower, column)

        def third_copy(which, half, chunk):
            src = sources[which].at[0, :, cols(half * HALF + chunk)]
            dst = auds[which].at[third_rows, cols(chunk)]
            return remote(
                src, dst, send_d.at[which, half * HALF + chunk], recv_third.at[which, chunk], half, before
            )

        def third_wait(which, chunk):
            dst = auds[which].at[third_rows, cols(chunk)]
            return remote(dst, dst, send_d.at[which, chunk], recv_third.at[which, chunk], tower, column)

        def pass_pair(which, chunk):
            part = mains[which].at[near_rows, cols(chunk)]
            return remote(part, part, send_a.at[which, chunk], recv_near.at[which, chunk], other, column)

        def pass_next(which, chunk):
            return remote(
                mains[which].at[near_rows, cols(chunk)],
                mains[which].at[next_rows, cols(chunk)],
                send_b.at[which, chunk],
                recv_next.at[which, chunk],
                0,
                after,
            )

        def part_copy(chunk):
            return remote(
                part_out.at[:, cols(chunk)],
                part_in.at[:, cols(own_base + chunk)],
                send_c.at[0, 1 + chunk],
                recv_part.at[own_base + chunk],
                3,
                column,
            )

        def stat_copy(chunk):
            return remote(
                part_stat.at[chunk],
                stat_in.at[own_base + chunk],
                send_c.at[1, 1 + chunk],
                recv_stat.at[own_base + chunk],
                3,
                column,
            )

        def pass_back(which, chunk):
            return remote(
                mains[which].at[near_rows, cols(chunk)],
                mains[which].at[next_rows, cols(chunk)],
                send_d.at[which, chunk],
                recv_next.at[which, chunk],
                2,
                before,
            )

        late = jnp.logical_and(tower == 0, past_edge)

        def edge_own(which):
            return pltpu.make_async_copy(sources[which].at[0], (edge_k, edge_v)[which], local_sem.at[5 + which])

        def edge_part(chunk):
            return remote(
                edge_out.at[:, cols(chunk)], edge_in.at[:, cols(chunk)], send_e.at[0, chunk], recv_edge.at[chunk], 3, edge
            )

        def edge_stats(chunk):
            return remote(
                edge_stat.at[chunk], edge_stat_in.at[chunk], send_e.at[1, chunk], recv_edge_stat.at[chunk], 3, edge
            )

        def pack(results):
            lane = lax.broadcasted_iota(jnp.int32, (BLOCK, DIM), 1)
            stat = jnp.zeros((BLOCK, DIM), jnp.float32)
            for i, (top, total) in enumerate(results):
                stat = jnp.where(lane == 2 * i, top, stat)
                stat = jnp.where(lane == 2 * i + 1, total, stat)
            return jnp.transpose(stat)[0:8]

        def attend_edge(chunk):
            dst = edge_q.at[:, cols(chunk)]
            remote(dst, dst, send_e.at[0, chunk], recv_edge_q.at[chunk], tower, column).wait_recv()
            results = []
            for i in range(PER):
                at = head_cols(chunk * PER + i)
                mixed, top, total = mix(edge_q[:, at], edge_k[:, at], edge_v[:, at], None)
                edge_out[:, at] = mixed.astype(jnp.bfloat16)
                results.append((top, total))
            edge_stat[chunk] = pack(results)
            edge_stats(chunk).start()
            edge_part(chunk).start()

        def relay_copy(which, chunk):
            return remote(
                (relay_k, relay_v)[which].at[:, cols(chunk)],
                mains[which].at[next_rows, cols(chunk)],
                send_e.at[which, chunk],
                recv_next.at[which, chunk],
                3,
                edge + 1,
            )

        def relay(chunk):
            for which in range(2):
                dst = (relay_k, relay_v)[which].at[:, cols(chunk)]
                remote(dst, dst, send_e.at[which, chunk], recv_relay.at[which, chunk], tower, column).wait_recv()
                relay_copy(which, chunk).start()

        for which in range(2):
            pair_copy(which).start()

        @pl.when(late)
        def _():
            for which in range(2):
                edge_own(which).start()
            for which in range(2):
                edge_own(which).wait()

        @pl.when(jnp.logical_and(tower == 0, has_back))
        def _():
            def start(chunk):
                for half in range(2):
                    for which in range(2):
                        third_copy(which, half, chunk).start()

            loop(HALF, start)

        for which in range(2):
            own_copy(which).start()

        @pl.when(jnp.logical_and(tower == 0, is_first))
        def _():
            for ref in mains:
                ref[BLOCK : 2 * BLOCK, :] = jnp.zeros((BLOCK, WIDTH), jnp.bfloat16)

        @pl.when(jnp.logical_not(has_forward))
        def _():
            for ref in auds:
                ref[2 * BLOCK : 3 * BLOCK, :] = jnp.zeros((BLOCK, WIDTH // 2), jnp.bfloat16)

        await_own()
        video_bias = bias_row(jnp.logical_and(column > 0, align_ref[1, before] > 3 * column), 2)
        audio_bias = bias_row(jnp.logical_and(has_forward, align_ref[1, column] > 3 * column + 3), 3)

        def video(step):
            @pl.when(tower == 0)
            def _():
                for base in (0, HALF):
                    chunk = base + step

                    @pl.when(jnp.logical_not(is_first))
                    def _():
                        await_next(chunk)

            await_near(other_base + step)

            @pl.when(tower == 0)
            def _():
                for base in (0, HALF):
                    video_heads(base + step, 2, video_bias)

            @pl.when(tower == 1)
            def _():
                for base in (0, HALF):
                    video_heads(base + step, 1, None)

        def take(step):
            chunk = own_base + step
            await_near(chunk)
            for which in range(2):
                pass_pair(which, chunk).start()

            @pl.when(has_forward)
            def _():
                for which in range(2):
                    pass_next(which, chunk).start()

            @pl.when(past_edge)
            def _():
                for which in range(2):
                    pass_back(which, chunk).start()

            @pl.when(jnp.logical_and(step > 0, jnp.logical_not(late)))
            def _():
                video(step - 1)

            @pl.when(late)
            def _():
                for i in range(2):
                    attend_edge(2 * step + i)

            @pl.when(jnp.logical_and(tower == 0, is_last))
            def _():
                for i in range(2):
                    relay(2 * step + i)

        loop(HALF, take)

        @pl.when(jnp.logical_not(late))
        def _():
            video(HALF - 1)

        for which in range(2):
            own_copy(which).wait()
            pair_wait(which).wait_recv()

        def audio(step):
            dst = aud_q.at[:, cols(step)]
            remote(dst, dst, send_a.at[0, step], recv_q.at[step], tower, column).wait_recv()

            @pl.when(has_forward)
            def _():
                for which in range(2):
                    third_wait(which, step).wait_recv()

            results = []
            for i in range(PER):
                at = head_cols(step * PER + i)
                mixed, top, total = mix(aud_q[:, at], aud_k[:, at], aud_v[:, at], audio_bias)
                part_out[:, at] = mixed.astype(jnp.bfloat16)
                results.append((top, total))
            part_stat[step] = pack(results)
            stat_copy(step).start()
            part_copy(step).start()

            @pl.when(late)
            def _():
                video(step)

        loop(HALF, audio)

        for which in range(2):
            pair_copy(which).wait_send()

        @pl.when(jnp.logical_and(tower == 0, has_back))
        def _():
            def drain(chunk):
                for half in range(2):
                    for which in range(2):
                        third_copy(which, half, chunk).wait_send()

            loop(HALF, drain)

        def drain(step):
            chunk = own_base + step
            for which in range(2):
                pass_pair(which, chunk).wait_send()

            @pl.when(has_forward)
            def _():
                for which in range(2):
                    pass_next(which, chunk).wait_send()

            @pl.when(past_edge)
            def _():
                for which in range(2):
                    pass_back(which, chunk).wait_send()

            stat_copy(step).wait_send()
            part_copy(step).wait_send()

        loop(HALF, drain)

        @pl.when(late)
        def _():
            def drain_edge(chunk):
                edge_part(chunk).wait_send()
                edge_stats(chunk).wait_send()

            loop(CHUNKS, drain_edge)

        @pl.when(jnp.logical_and(tower == 0, is_last))
        def _():
            def drain_relay(chunk):
                for which in range(2):
                    relay_copy(which, chunk).wait_send()

            loop(CHUNKS, drain_relay)

        loop(CHUNKS, finish_out)

    @pl.when(tower == 2)
    def _():
        def near_copy(which, chunk):
            return remote(
                sources[which].at[0, :, cols(chunk)],
                mains[which].at[near_rows, cols(chunk)],
                send_a.at[which, chunk],
                recv_near.at[which, chunk],
                3,
                column,
            )

        def next_copy(which, chunk):
            return remote(
                sources[which].at[0, :, cols(chunk)],
                mains[which].at[next_rows, cols(chunk)],
                send_b.at[which, chunk],
                recv_next.at[which, chunk],
                3,
                after,
            )

        def start_near(chunk):
            for which in range(2):
                near_copy(which, chunk).start()

        def start_next(chunk):
            for which in range(2):
                next_copy(which, chunk).start()

        def relay_in(which, chunk):
            return remote(
                sources[which].at[0, :, cols(chunk)],
                (relay_k, relay_v)[which].at[:, cols(chunk)],
                send_b.at[which, chunk],
                recv_relay.at[which, chunk],
                0,
                last,
            )

        @pl.when(has_forward)
        def _():
            loop(CHUNKS, start_next)

        @pl.when(at_edge)
        def _():
            def start_relay(chunk):
                for which in range(2):
                    relay_in(which, chunk).start()

            loop(CHUNKS, start_relay)

        loop(CHUNKS, start_near)

        @pl.when(is_last)
        def _():
            for ref in mains:
                ref[BLOCK : 2 * BLOCK, :] = jnp.zeros((BLOCK, WIDTH), jnp.bfloat16)

        await_own()
        linked = jnp.logical_and(column < seq_count - 1, align_ref[0, after] <= 3 * column + 2)
        bias = bias_row(linked, 2)

        def video(chunk):
            await_near(chunk)

            @pl.when(jnp.logical_not(is_last))
            def _():
                await_next(chunk)

            video_heads(chunk, 2, bias)

        loop(CHUNKS, video)

        def drain(chunk):
            for which in range(2):
                near_copy(which, chunk).wait_send()

            @pl.when(has_forward)
            def _():
                for which in range(2):
                    next_copy(which, chunk).wait_send()

            @pl.when(at_edge)
            def _():
                for which in range(2):
                    relay_in(which, chunk).wait_send()

            finish_out(chunk)

        loop(CHUNKS, drain)

    @pl.when(tower == 3)
    def _():
        def far_copy(which, half, step):
            chunk = half * HALF + step
            return remote(
                sources[which].at[0, :, cols(chunk)],
                mains[which].at[near_rows, cols(chunk)],
                send_a.at[which, chunk],
                recv_near.at[which, chunk],
                half,
                column,
            )

        def query_copy(half, step):
            return remote(
                q_hbm.at[0, :, cols(half * HALF + step)],
                aud_q.at[:, cols(step)],
                send_d.at[half, step],
                recv_q.at[step],
                half,
                column,
            )

        def near_copy(which, chunk):
            return remote(
                sources[which].at[0, :, cols(chunk)],
                mains[which].at[near_rows, cols(chunk)],
                send_b.at[which, chunk],
                recv_near.at[which, chunk],
                2,
                column,
            )

        def back_copy(which, chunk):
            return remote(
                sources[which].at[0, :, cols(chunk)],
                mains[which].at[next_rows, cols(chunk)],
                send_c.at[which, chunk],
                recv_next.at[which, chunk],
                2,
                before,
            )

        def start_far(step):
            for half in range(2):
                for which in range(2):
                    far_copy(which, half, step).start()

        loop(HALF, start_far)

        def start_query(step):
            for half in range(2):
                query_copy(half, step).start()

        loop(HALF, start_query)

        def edge_query(chunk):
            return remote(
                q_hbm.at[0, :, cols(chunk)],
                edge_q.at[:, cols(chunk)],
                send_e.at[0, chunk],
                recv_edge_q.at[chunk],
                0,
                edge + 1,
            )

        def edge_copy(which, chunk):
            return remote(
                sources[which].at[0, :, cols(chunk)],
                mains[which].at[next_rows, cols(chunk)],
                send_e.at[1 + which, chunk],
                recv_next.at[which, chunk],
                0,
                edge + 1,
            )

        @pl.when(at_edge)
        def _():
            def start_queries(chunk):
                edge_query(chunk).start()

            loop(CHUNKS, start_queries)

            def start_edge(step):
                for half in range(2):
                    for which in range(2):
                        edge_copy(which, half * HALF + step).start()

            loop(HALF, start_edge)

        @pl.when(has_back)
        def _():
            def start_back(chunk):
                for which in range(2):
                    back_copy(which, chunk).start()

            loop(CHUNKS, start_back)

        def start_near(chunk):
            for which in range(2):
                near_copy(which, chunk).start()

        loop(CHUNKS, start_near)

        @pl.when(is_first)
        def _():
            for ref in mains:
                ref[BLOCK : 2 * BLOCK, :] = jnp.zeros((BLOCK, WIDTH), jnp.bfloat16)

        await_own()
        bias = bias_row(align_ref[0, column] <= 3 * column - 1, 2)

        def local(chunk):
            await_near(chunk)

            @pl.when(jnp.logical_not(is_first))
            def _():
                await_next(chunk)

            for i in range(PER):
                head = chunk * PER + i
                at = head_cols(head)
                mixed, top, total = mix(q_own[:, at], main_k[:, at], main_v[:, at], bias)
                local_mix[:, at] = mixed
                local_top[head] = jnp.broadcast_to(top, (BLOCK, DIM))
                local_total[head] = jnp.broadcast_to(total, (BLOCK, DIM))

        loop(CHUNKS, local)

        def unpack(rows):
            stat = jnp.concatenate([rows, jnp.zeros((DIM - 8, BLOCK), jnp.float32)], axis=0)
            return jnp.transpose(stat)

        @pl.when(at_edge)
        def _():
            reach = align_ref[1, column] > 3 * column + 3
            shift = jnp.where(reach, 0.0, -jnp.inf).astype(jnp.float32)

            def add_edge(chunk):
                dst = edge_stat_in.at[chunk]
                remote(dst, dst, send_a.at[0, chunk], recv_edge_stat.at[chunk], tower, column).wait_recv()
                dst = edge_in.at[:, cols(chunk)]
                remote(dst, dst, send_a.at[0, chunk], recv_edge.at[chunk], tower, column).wait_recv()
                stat = unpack(edge_stat_in[chunk])
                for i in range(PER):
                    head = chunk * PER + i
                    at = head_cols(head)
                    far_top = stat[:, 2 * i : 2 * i + 1] + shift
                    near_top = local_top[head][:, 0:1]
                    top = jnp.maximum(far_top, near_top)
                    far = jnp.exp2((far_top - top) * COLD)
                    near = jnp.exp2((near_top - top) * COLD)
                    total = far * stat[:, 2 * i + 1 : 2 * i + 2] + near * local_total[head][:, 0:1]
                    local_mix[:, at] = edge_in[:, at].astype(jnp.float32) * far + local_mix[:, at] * near
                    local_top[head] = jnp.broadcast_to(top, (BLOCK, DIM))
                    local_total[head] = jnp.broadcast_to(total, (BLOCK, DIM))

            loop(CHUNKS, add_edge)

        def merge_chunk(chunk):
            dst = stat_in.at[chunk]
            remote(dst, dst, send_a.at[0, chunk], recv_stat.at[chunk], tower, column).wait_recv()
            dst = part_in.at[:, cols(chunk)]
            remote(dst, dst, send_a.at[0, chunk], recv_part.at[chunk], tower, column).wait_recv()
            stat = unpack(stat_in[chunk])
            for i in range(PER):
                head = chunk * PER + i
                at = head_cols(head)
                far_top = stat[:, 2 * i : 2 * i + 1]
                far_total = stat[:, 2 * i + 1 : 2 * i + 2]
                near_top = local_top[head][:, 0:1]
                near_total = local_total[head][:, 0:1]
                top = jnp.maximum(far_top, near_top)
                far = jnp.exp2((far_top - top) * COLD)
                near = jnp.exp2((near_top - top) * COLD)
                scale = gate_ref[1, head] / (far * far_total + near * near_total)
                mixed = part_in[:, at].astype(jnp.float32) * (far * scale) + local_mix[:, at] * (near * scale)
                out_buf[:, at] = mixed.astype(jnp.bfloat16)
            write_out(chunk).start()

        def merge(step):
            for half in range(2):
                merge_chunk(half * HALF + step)

        loop(HALF, merge)

        def drain_far(step):
            for half in range(2):
                for which in range(2):
                    far_copy(which, half, step).wait_send()
                query_copy(half, step).wait_send()

        loop(HALF, drain_far)

        def drain(chunk):
            for which in range(2):
                near_copy(which, chunk).wait_send()

            @pl.when(has_back)
            def _():
                for which in range(2):
                    back_copy(which, chunk).wait_send()

            @pl.when(at_edge)
            def _():
                edge_query(chunk).wait_send()
                for which in range(2):
                    edge_copy(which, chunk).wait_send()

            finish_out(chunk)

        loop(CHUNKS, drain)


def local(seq_count, queries, keys, values, alignment, cross_gate):
    bf16, f32 = jnp.bfloat16, jnp.float32
    dma = pltpu.SemaphoreType.DMA
    any_space = pl.BlockSpec(memory_space=pl.ANY)
    block = pltpu.VMEM((BLOCK, WIDTH), bf16)
    hbm = pl.BlockSpec(memory_space=pltpu.HBM)
    return pl.pallas_call(
        functools.partial(kernel, seq_count),
        out_shape=jax.ShapeDtypeStruct(queries.shape, bf16),
        in_specs=[hbm] * 5,
        out_specs=any_space,
        scratch_shapes=[
            pltpu.VMEM((BLOCK, WIDTH), bf16),
            pltpu.VMEM((2 * BLOCK, WIDTH), bf16),
            pltpu.VMEM((2 * BLOCK, WIDTH), bf16),
            pltpu.VMEM((BLOCK, WIDTH // 2), bf16),
            pltpu.VMEM((3 * BLOCK, WIDTH // 2), bf16),
            pltpu.VMEM((3 * BLOCK, WIDTH // 2), bf16),
            pltpu.VMEM((BLOCK, WIDTH // 2), bf16),
            pltpu.VMEM((HALF, 8, BLOCK), f32),
            pltpu.VMEM((BLOCK, WIDTH), bf16),
            pltpu.VMEM((CHUNKS, 8, BLOCK), f32),
            pltpu.VMEM((BLOCK, WIDTH), f32),
            pltpu.VMEM((HEADS, BLOCK, DIM), f32),
            pltpu.VMEM((HEADS, BLOCK, DIM), f32),
            pltpu.VMEM((BLOCK, WIDTH), bf16),
            pltpu.SMEM(alignment.shape[::-1], jnp.int32),
            pltpu.SMEM(cross_gate.shape, f32),
            block,
            block,
            block,
            block,
            pltpu.VMEM((CHUNKS, 8, BLOCK), f32),
            block,
            pltpu.VMEM((CHUNKS, 8, BLOCK), f32),
            block,
            block,
            dma((7,)),
            dma((CHUNKS,)),
            dma((2, CHUNKS)),
            dma((2, CHUNKS)),
            dma((2, CHUNKS)),
            dma((2, CHUNKS)),
            dma((2, CHUNKS)),
            dma((2, CHUNKS)),
            dma((HALF,)),
            dma((2,)),
            dma((2, HALF)),
            dma((CHUNKS,)),
            dma((CHUNKS,)),
            dma((3, CHUNKS)),
            dma((CHUNKS,)),
            dma((CHUNKS,)),
            dma((CHUNKS,)),
            dma((2, CHUNKS)),
        ],
        compiler_params=pltpu.CompilerParams(
            collective_id=0, has_side_effects=True, vmem_limit_bytes=52000000
        ),
    )(*(pltpu.with_memory_space_constraint(a, pltpu.HBM) for a in (jnp.transpose(alignment), cross_gate, queries, keys, values)))


def solution(mesh):
    placed = (P("tower", "seq", None), P("tower", "seq", None), P("tower", "seq", None), P(), P())
    return jax.shard_map(
        functools.partial(local, mesh.shape["seq"]),
        mesh=mesh,
        in_specs=placed,
        out_specs=P("tower", "seq", None),
        check_vma=False,
    )
```

```python
import functools
import math

import jax
import jax.numpy as jnp
from jax import lax
from jax.experimental import pallas as pl
from jax.experimental.pallas import tpu as pltpu
from jax.sharding import PartitionSpec as P

HEADS = 24
DIM = 128
BLOCK = 128
WIDTH = HEADS * DIM
PER = 2
CHUNKS = HEADS // PER
HALF = CHUNKS // 2
SPAN = PER * DIM
COLD = math.log2(math.e) / math.sqrt(DIM)
MESH = pl.DeviceIdType.MESH


def cols(chunk):
    return pl.ds(pl.multiple_of(chunk * SPAN, SPAN), SPAN)


def head_cols(head):
    return pl.ds(pl.multiple_of(head * DIM, DIM), DIM)


def loop(count, body):
    def step(i, carry):
        body(i)
        return carry

    lax.fori_loop(0, count, step, 0)


def mix(q, k, v, bias):
    scores = lax.dot_general(q, k, (((1,), (1,)), ((), ())), preferred_element_type=jnp.float32)
    if bias is not None:
        scores = scores + bias
    top = jnp.max(scores, axis=1, keepdims=True)
    weights = jnp.exp2((scores - top) * COLD)
    total = jnp.sum(weights, axis=1, keepdims=True)
    mixed = jnp.dot(weights.astype(jnp.bfloat16), v, preferred_element_type=jnp.float32)
    return mixed, top, total


def bias_row(linked, blocks):
    off = jnp.where(linked, 0.0, -jnp.inf).astype(jnp.float32)
    place = lax.broadcasted_iota(jnp.int32, (1, blocks * BLOCK), 1)
    return jnp.where(place >= (blocks - 1) * BLOCK, off, 0.0)


def kernel(
    seq_count,
    align_hbm,
    gate_hbm,
    q_hbm,
    k_hbm,
    v_hbm,
    out_hbm,
    q_own,
    main_k,
    main_v,
    aud_q,
    aud_k,
    aud_v,
    part_out,
    part_stat,
    part_in,
    stat_in,
    local_mix,
    local_top,
    local_total,
    out_buf,
    align_ref,
    gate_ref,
    edge_k,
    edge_v,
    edge_q,
    edge_out,
    edge_stat,
    edge_in,
    edge_stat_in,
    relay_k,
    relay_v,
    local_sem,
    out_sem,
    send_a,
    send_b,
    send_c,
    send_d,
    recv_near,
    recv_next,
    recv_q,
    recv_pair,
    recv_third,
    recv_part,
    recv_stat,
    send_e,
    recv_edge_q,
    recv_edge,
    recv_edge_stat,
    recv_relay,
):
    tower = lax.axis_index("tower")
    column = lax.axis_index("seq")
    is_first = column == 0
    is_last = column == seq_count - 1
    edge = seq_count // 2 - 1
    last = seq_count - 1
    at_edge = column == edge
    past_edge = column == edge + 1
    before = jnp.maximum(column - 1, 0)
    after = jnp.minimum(column + 1, seq_count - 1)
    sources = (k_hbm, v_hbm)
    mains = (main_k, main_v)
    auds = (aud_k, aud_v)

    def device(t, c):
        return {"tower": t, "seq": c}

    def remote(src, dst, send, recv, t, c):
        return pltpu.make_async_remote_copy(
            src_ref=src, dst_ref=dst, send_sem=send, recv_sem=recv, device_id=device(t, c), device_id_type=MESH
        )

    q_copy = pltpu.make_async_copy(q_hbm.at[0], q_own, local_sem.at[2])
    q_copy.start()
    small = (
        pltpu.make_async_copy(align_hbm, align_ref, local_sem.at[3]),
        pltpu.make_async_copy(gate_hbm, gate_ref, local_sem.at[4]),
    )
    for copy in small:
        copy.start()

    barrier = pltpu.get_barrier_semaphore()

    def greet(t, c):
        pl.semaphore_signal(barrier, inc=1, device_id=device(t, c), device_id_type=MESH)

    def meet(fixed, others):
        peers = jnp.int32(len(fixed))
        for t in fixed:
            greet(t, column)
        for when, t, c in others:

            @pl.when(when)
            def _():
                greet(t, c)

            peers = peers + jnp.where(when, 1, 0)
        pl.semaphore_wait(barrier, peers)

    has_back = jnp.logical_not(jnp.logical_or(is_first, past_edge))
    has_forward = jnp.logical_not(jnp.logical_or(is_last, at_edge))

    @pl.when(tower == 0)
    def _():
        meet(
            (1, 3),
            [
                (has_back, 0, before),
                (has_back, 1, before),
                (has_forward, 0, after),
                (past_edge, 2, edge),
                (past_edge, 3, edge),
                (is_last, 2, edge),
                (is_last, 3, edge + 1),
            ],
        )

    @pl.when(tower == 1)
    def _():
        meet((0, 3), [(has_forward, 0, after), (past_edge, 2, edge)])

    @pl.when(tower == 2)
    def _():
        meet((3,), [(has_forward, 3, after), (at_edge, 0, edge + 1), (at_edge, 1, edge + 1), (at_edge, 0, last)])

    @pl.when(tower == 3)
    def _():
        meet((0, 1, 2), [(has_back, 2, before), (at_edge, 0, edge + 1), (past_edge, 0, last)])

    near_rows = pl.ds(0, BLOCK)
    next_rows = pl.ds(BLOCK, BLOCK)
    third_rows = pl.ds(2 * BLOCK, BLOCK)

    def await_own():
        q_copy.wait()
        for copy in small:
            copy.wait()

    def write_out(chunk):
        return pltpu.make_async_copy(
            out_buf.at[:, cols(chunk)], out_hbm.at[0, :, cols(chunk)], out_sem.at[chunk]
        )

    def recv_main(which, chunk, rows, sems):
        dst = mains[which].at[rows, cols(chunk)]
        return remote(dst, dst, send_a.at[which, chunk], sems.at[which, chunk], tower, column)

    def await_near(chunk):
        for which in range(2):
            recv_main(which, chunk, near_rows, recv_near).wait_recv()

    def await_next(chunk):
        for which in range(2):
            recv_main(which, chunk, next_rows, recv_next).wait_recv()

    def video_heads(chunk, blocks, bias):
        for i in range(PER):
            head = chunk * PER + i
            at = head_cols(head)
            mixed, _, total = mix(
                q_own[:, at], main_k[0 : blocks * BLOCK, at], main_v[0 : blocks * BLOCK, at], bias
            )
            out_buf[:, at] = (mixed * (gate_ref[0, head] / total)).astype(jnp.bfloat16)
        write_out(chunk).start()

    def finish_out(chunk):
        write_out(chunk).wait()

    @pl.when(tower < 2)
    def _():
        other = 1 - tower
        own_base = tower * HALF
        other_base = other * HALF
        own_rows = pl.ds(pl.multiple_of(tower * BLOCK, BLOCK), BLOCK)
        half_cols = pl.ds(pl.multiple_of(own_base * SPAN, SPAN), HALF * SPAN)
        other_cols = pl.ds(pl.multiple_of(other_base * SPAN, SPAN), HALF * SPAN)
        pair_rows = pl.ds(pl.multiple_of(other * BLOCK, BLOCK), BLOCK)

        def own_copy(which):
            return pltpu.make_async_copy(
                sources[which].at[0, :, half_cols], auds[which].at[own_rows, :], local_sem.at[which]
            )

        def pair_copy(which):
            return remote(
                sources[which].at[0, :, other_cols],
                auds[which].at[own_rows, :],
                send_c.at[which, 0],
                recv_pair.at[which],
                other,
                column,
            )

        def pair_wait(which):
            dst = auds[which].at[pair_rows, :]
            return remote(dst, dst, send_c.at[which, 0], recv_pair.at[which], tower, column)

        def third_copy(which, half, chunk):
            src = sources[which].at[0, :, cols(half * HALF + chunk)]
            dst = auds[which].at[third_rows, cols(chunk)]
            return remote(
                src, dst, send_d.at[which, half * HALF + chunk], recv_third.at[which, chunk], half, before
            )

        def third_wait(which, chunk):
            dst = auds[which].at[third_rows, cols(chunk)]
            return remote(dst, dst, send_d.at[which, chunk], recv_third.at[which, chunk], tower, column)

        def pass_pair(which, chunk):
            part = mains[which].at[near_rows, cols(chunk)]
            return remote(part, part, send_a.at[which, chunk], recv_near.at[which, chunk], other, column)

        def pass_next(which, chunk):
            return remote(
                mains[which].at[near_rows, cols(chunk)],
                mains[which].at[next_rows, cols(chunk)],
                send_b.at[which, chunk],
                recv_next.at[which, chunk],
                0,
                after,
            )

        def part_copy(chunk):
            return remote(
                part_out.at[:, cols(chunk)],
                part_in.at[:, cols(own_base + chunk)],
                send_c.at[0, 1 + chunk],
                recv_part.at[own_base + chunk],
                3,
                column,
            )

        def stat_copy(chunk):
            return remote(
                part_stat.at[chunk],
                stat_in.at[own_base + chunk],
                send_c.at[1, 1 + chunk],
                recv_stat.at[own_base + chunk],
                3,
                column,
            )

        def pass_back(which, chunk):
            return remote(
                mains[which].at[near_rows, cols(chunk)],
                mains[which].at[next_rows, cols(chunk)],
                send_d.at[which, chunk],
                recv_next.at[which, chunk],
                2,
                before,
            )

        late = jnp.logical_and(tower == 0, past_edge)

        def edge_own(which):
            return pltpu.make_async_copy(sources[which].at[0], (edge_k, edge_v)[which], local_sem.at[5 + which])

        def edge_part(chunk):
            return remote(
                edge_out.at[:, cols(chunk)], edge_in.at[:, cols(chunk)], send_e.at[0, chunk], recv_edge.at[chunk], 3, edge
            )

        def edge_stats(chunk):
            return remote(
                edge_stat.at[chunk], edge_stat_in.at[chunk], send_e.at[1, chunk], recv_edge_stat.at[chunk], 3, edge
            )

        def pack(results):
            lane = lax.broadcasted_iota(jnp.int32, (BLOCK, DIM), 1)
            stat = jnp.zeros((BLOCK, DIM), jnp.float32)
            for i, (top, total) in enumerate(results):
                stat = jnp.where(lane == 2 * i, top, stat)
                stat = jnp.where(lane == 2 * i + 1, total, stat)
            return jnp.transpose(stat)[0:8]

        def attend_edge(chunk):
            dst = edge_q.at[:, cols(chunk)]
            remote(dst, dst, send_e.at[0, chunk], recv_edge_q.at[chunk], tower, column).wait_recv()
            results = []
            for i in range(PER):
                at = head_cols(chunk * PER + i)
                mixed, top, total = mix(edge_q[:, at], edge_k[:, at], edge_v[:, at], None)
                edge_out[:, at] = mixed.astype(jnp.bfloat16)
                results.append((top, total))
            edge_stat[chunk] = pack(results)
            edge_stats(chunk).start()
            edge_part(chunk).start()

        def relay_copy(which, chunk):
            return remote(
                (relay_k, relay_v)[which].at[:, cols(chunk)],
                mains[which].at[next_rows, cols(chunk)],
                send_e.at[which, chunk],
                recv_next.at[which, chunk],
                3,
                edge + 1,
            )

        def relay(chunk):
            for which in range(2):
                dst = (relay_k, relay_v)[which].at[:, cols(chunk)]
                remote(dst, dst, send_e.at[which, chunk], recv_relay.at[which, chunk], tower, column).wait_recv()
                relay_copy(which, chunk).start()

        for which in range(2):
            pair_copy(which).start()

        @pl.when(late)
        def _():
            for which in range(2):
                edge_own(which).start()
            for which in range(2):
                edge_own(which).wait()

        @pl.when(jnp.logical_and(tower == 0, has_back))
        def _():
            def start(chunk):
                for half in range(2):
                    for which in range(2):
                        third_copy(which, half, chunk).start()

            loop(HALF, start)

        for which in range(2):
            own_copy(which).start()

        @pl.when(jnp.logical_and(tower == 0, is_first))
        def _():
            for ref in mains:
                ref[BLOCK : 2 * BLOCK, :] = jnp.zeros((BLOCK, WIDTH), jnp.bfloat16)

        @pl.when(jnp.logical_not(has_forward))
        def _():
            for ref in auds:
                ref[2 * BLOCK : 3 * BLOCK, :] = jnp.zeros((BLOCK, WIDTH // 2), jnp.bfloat16)

        await_own()
        video_bias = bias_row(jnp.logical_and(column > 0, align_ref[1, before] > 3 * column), 2)
        audio_bias = bias_row(jnp.logical_and(has_forward, align_ref[1, column] > 3 * column + 3), 3)

        def video(step):
            @pl.when(tower == 0)
            def _():
                for base in (0, HALF):
                    chunk = base + step

                    @pl.when(jnp.logical_not(is_first))
                    def _():
                        await_next(chunk)

            await_near(other_base + step)

            @pl.when(tower == 0)
            def _():
                for base in (0, HALF):
                    video_heads(base + step, 2, video_bias)

            @pl.when(tower == 1)
            def _():
                for base in (0, HALF):
                    video_heads(base + step, 1, None)

        def take(step):
            chunk = own_base + step
            await_near(chunk)
            for which in range(2):
                pass_pair(which, chunk).start()

            @pl.when(has_forward)
            def _():
                for which in range(2):
                    pass_next(which, chunk).start()

            @pl.when(past_edge)
            def _():
                for which in range(2):
                    pass_back(which, chunk).start()

            @pl.when(jnp.logical_and(tower == 0, is_last))
            def _():
                for i in range(2):
                    relay(2 * step + i)

            @pl.when(step > 0)
            def _():
                @pl.when(jnp.logical_not(late))
                def _():
                    video(step - 1)

                audio(step - 1)

            @pl.when(late)
            def _():
                for i in range(2):
                    attend_edge(2 * step + i)

        def audio(step):
            dst = aud_q.at[:, cols(step)]
            remote(dst, dst, send_a.at[0, step], recv_q.at[step], tower, column).wait_recv()

            @pl.when(has_forward)
            def _():
                for which in range(2):
                    third_wait(which, step).wait_recv()

            results = []
            for i in range(PER):
                at = head_cols(step * PER + i)
                mixed, top, total = mix(aud_q[:, at], aud_k[:, at], aud_v[:, at], audio_bias)
                part_out[:, at] = mixed.astype(jnp.bfloat16)
                results.append((top, total))
            part_stat[step] = pack(results)
            stat_copy(step).start()
            part_copy(step).start()

        for which in range(2):
            own_copy(which).wait()
            pair_wait(which).wait_recv()

        loop(HALF, take)
        audio(HALF - 1)

        def rest(step, carry):
            video(step)
            return carry

        lax.fori_loop(jnp.where(late, 0, HALF - 1), HALF, rest, 0)

        for which in range(2):
            pair_copy(which).wait_send()

        @pl.when(jnp.logical_and(tower == 0, has_back))
        def _():
            def drain(chunk):
                for half in range(2):
                    for which in range(2):
                        third_copy(which, half, chunk).wait_send()

            loop(HALF, drain)

        def drain(step):
            chunk = own_base + step
            for which in range(2):
                pass_pair(which, chunk).wait_send()

            @pl.when(has_forward)
            def _():
                for which in range(2):
                    pass_next(which, chunk).wait_send()

            @pl.when(past_edge)
            def _():
                for which in range(2):
                    pass_back(which, chunk).wait_send()

            stat_copy(step).wait_send()
            part_copy(step).wait_send()

        loop(HALF, drain)

        @pl.when(late)
        def _():
            def drain_edge(chunk):
                edge_part(chunk).wait_send()
                edge_stats(chunk).wait_send()

            loop(CHUNKS, drain_edge)

        @pl.when(jnp.logical_and(tower == 0, is_last))
        def _():
            def drain_relay(chunk):
                for which in range(2):
                    relay_copy(which, chunk).wait_send()

            loop(CHUNKS, drain_relay)

        loop(CHUNKS, finish_out)

    @pl.when(tower == 2)
    def _():
        def near_copy(which, chunk):
            return remote(
                sources[which].at[0, :, cols(chunk)],
                mains[which].at[near_rows, cols(chunk)],
                send_a.at[which, chunk],
                recv_near.at[which, chunk],
                3,
                column,
            )

        def next_copy(which, chunk):
            return remote(
                sources[which].at[0, :, cols(chunk)],
                mains[which].at[next_rows, cols(chunk)],
                send_b.at[which, chunk],
                recv_next.at[which, chunk],
                3,
                after,
            )

        def start_near(chunk):
            for which in range(2):
                near_copy(which, chunk).start()

        def start_next(chunk):
            for which in range(2):
                next_copy(which, chunk).start()

        def relay_in(which, chunk):
            return remote(
                sources[which].at[0, :, cols(chunk)],
                (relay_k, relay_v)[which].at[:, cols(chunk)],
                send_b.at[which, chunk],
                recv_relay.at[which, chunk],
                0,
                last,
            )

        @pl.when(has_forward)
        def _():
            loop(CHUNKS, start_next)

        @pl.when(at_edge)
        def _():
            def start_relay(chunk):
                for which in range(2):
                    relay_in(which, chunk).start()

            loop(CHUNKS, start_relay)

        loop(CHUNKS, start_near)

        @pl.when(is_last)
        def _():
            for ref in mains:
                ref[BLOCK : 2 * BLOCK, :] = jnp.zeros((BLOCK, WIDTH), jnp.bfloat16)

        await_own()
        linked = jnp.logical_and(column < seq_count - 1, align_ref[0, after] <= 3 * column + 2)
        bias = bias_row(linked, 2)

        def video(chunk):
            await_near(chunk)

            @pl.when(jnp.logical_not(is_last))
            def _():
                await_next(chunk)

            video_heads(chunk, 2, bias)

        loop(CHUNKS, video)

        def drain(chunk):
            for which in range(2):
                near_copy(which, chunk).wait_send()

            @pl.when(has_forward)
            def _():
                for which in range(2):
                    next_copy(which, chunk).wait_send()

            @pl.when(at_edge)
            def _():
                for which in range(2):
                    relay_in(which, chunk).wait_send()

            finish_out(chunk)

        loop(CHUNKS, drain)

    @pl.when(tower == 3)
    def _():
        def far_copy(which, half, step):
            chunk = half * HALF + step
            return remote(
                sources[which].at[0, :, cols(chunk)],
                mains[which].at[near_rows, cols(chunk)],
                send_a.at[which, chunk],
                recv_near.at[which, chunk],
                half,
                column,
            )

        def query_copy(half, step):
            return remote(
                q_hbm.at[0, :, cols(half * HALF + step)],
                aud_q.at[:, cols(step)],
                send_d.at[half, step],
                recv_q.at[step],
                half,
                column,
            )

        def near_copy(which, chunk):
            return remote(
                sources[which].at[0, :, cols(chunk)],
                mains[which].at[near_rows, cols(chunk)],
                send_b.at[which, chunk],
                recv_near.at[which, chunk],
                2,
                column,
            )

        def back_copy(which, chunk):
            return remote(
                sources[which].at[0, :, cols(chunk)],
                mains[which].at[next_rows, cols(chunk)],
                send_c.at[which, chunk],
                recv_next.at[which, chunk],
                2,
                before,
            )

        def edge_query(chunk):
            return remote(
                q_hbm.at[0, :, cols(chunk)],
                edge_q.at[:, cols(chunk)],
                send_e.at[0, chunk],
                recv_edge_q.at[chunk],
                0,
                edge + 1,
            )

        def edge_copy(which, chunk):
            return remote(
                sources[which].at[0, :, cols(chunk)],
                mains[which].at[next_rows, cols(chunk)],
                send_e.at[1 + which, chunk],
                recv_next.at[which, chunk],
                0,
                edge + 1,
            )

        @pl.when(at_edge)
        def _():
            def start_queries(chunk):
                edge_query(chunk).start()

            loop(CHUNKS, start_queries)

        def start_far(step):
            for half in range(2):
                for which in range(2):
                    far_copy(which, half, step).start()

            @pl.when(step > 0)
            def _():
                for half in range(2):
                    query_copy(half, step - 1).start()

        loop(HALF, start_far)
        for half in range(2):
            query_copy(half, HALF - 1).start()

        @pl.when(at_edge)
        def _():
            def start_edge(step):
                for half in range(2):
                    for which in range(2):
                        edge_copy(which, half * HALF + step).start()

            loop(HALF, start_edge)

        @pl.when(has_back)
        def _():
            def start_back(chunk):
                for which in range(2):
                    back_copy(which, chunk).start()

            loop(CHUNKS, start_back)

        def start_near(chunk):
            for which in range(2):
                near_copy(which, chunk).start()

        loop(CHUNKS, start_near)

        @pl.when(is_first)
        def _():
            for ref in mains:
                ref[BLOCK : 2 * BLOCK, :] = jnp.zeros((BLOCK, WIDTH), jnp.bfloat16)

        await_own()
        bias = bias_row(align_ref[0, column] <= 3 * column - 1, 2)

        def local(chunk):
            await_near(chunk)

            @pl.when(jnp.logical_not(is_first))
            def _():
                await_next(chunk)

            for i in range(PER):
                head = chunk * PER + i
                at = head_cols(head)
                mixed, top, total = mix(q_own[:, at], main_k[:, at], main_v[:, at], bias)
                local_mix[:, at] = mixed
                local_top[head] = jnp.broadcast_to(top, (BLOCK, DIM))
                local_total[head] = jnp.broadcast_to(total, (BLOCK, DIM))

        loop(CHUNKS, local)

        def unpack(rows):
            stat = jnp.concatenate([rows, jnp.zeros((DIM - 8, BLOCK), jnp.float32)], axis=0)
            return jnp.transpose(stat)

        @pl.when(at_edge)
        def _():
            reach = align_ref[1, column] > 3 * column + 3
            shift = jnp.where(reach, 0.0, -jnp.inf).astype(jnp.float32)

            def add_edge(chunk):
                dst = edge_stat_in.at[chunk]
                remote(dst, dst, send_a.at[0, chunk], recv_edge_stat.at[chunk], tower, column).wait_recv()
                dst = edge_in.at[:, cols(chunk)]
                remote(dst, dst, send_a.at[0, chunk], recv_edge.at[chunk], tower, column).wait_recv()
                stat = unpack(edge_stat_in[chunk])
                for i in range(PER):
                    head = chunk * PER + i
                    at = head_cols(head)
                    far_top = stat[:, 2 * i : 2 * i + 1] + shift
                    near_top = local_top[head][:, 0:1]
                    top = jnp.maximum(far_top, near_top)
                    far = jnp.exp2((far_top - top) * COLD)
                    near = jnp.exp2((near_top - top) * COLD)
                    total = far * stat[:, 2 * i + 1 : 2 * i + 2] + near * local_total[head][:, 0:1]
                    local_mix[:, at] = edge_in[:, at].astype(jnp.float32) * far + local_mix[:, at] * near
                    local_top[head] = jnp.broadcast_to(top, (BLOCK, DIM))
                    local_total[head] = jnp.broadcast_to(total, (BLOCK, DIM))

            loop(CHUNKS, add_edge)

        def merge_chunk(chunk):
            dst = stat_in.at[chunk]
            remote(dst, dst, send_a.at[0, chunk], recv_stat.at[chunk], tower, column).wait_recv()
            dst = part_in.at[:, cols(chunk)]
            remote(dst, dst, send_a.at[0, chunk], recv_part.at[chunk], tower, column).wait_recv()
            stat = unpack(stat_in[chunk])
            for i in range(PER):
                head = chunk * PER + i
                at = head_cols(head)
                far_top = stat[:, 2 * i : 2 * i + 1]
                far_total = stat[:, 2 * i + 1 : 2 * i + 2]
                near_top = local_top[head][:, 0:1]
                near_total = local_total[head][:, 0:1]
                top = jnp.maximum(far_top, near_top)
                far = jnp.exp2((far_top - top) * COLD)
                near = jnp.exp2((near_top - top) * COLD)
                scale = gate_ref[1, head] / (far * far_total + near * near_total)
                mixed = part_in[:, at].astype(jnp.float32) * (far * scale) + local_mix[:, at] * (near * scale)
                out_buf[:, at] = mixed.astype(jnp.bfloat16)
            write_out(chunk).start()

        def merge(step):
            for half in range(2):
                merge_chunk(half * HALF + step)

        loop(HALF, merge)

        def drain_far(step):
            for half in range(2):
                for which in range(2):
                    far_copy(which, half, step).wait_send()
                query_copy(half, step).wait_send()

        loop(HALF, drain_far)

        def drain(chunk):
            for which in range(2):
                near_copy(which, chunk).wait_send()

            @pl.when(has_back)
            def _():
                for which in range(2):
                    back_copy(which, chunk).wait_send()

            @pl.when(at_edge)
            def _():
                edge_query(chunk).wait_send()
                for which in range(2):
                    edge_copy(which, chunk).wait_send()

            finish_out(chunk)

        loop(CHUNKS, drain)


def local(seq_count, queries, keys, values, alignment, cross_gate):
    bf16, f32 = jnp.bfloat16, jnp.float32
    dma = pltpu.SemaphoreType.DMA
    any_space = pl.BlockSpec(memory_space=pl.ANY)
    block = pltpu.VMEM((BLOCK, WIDTH), bf16)
    hbm = pl.BlockSpec(memory_space=pltpu.HBM)
    return pl.pallas_call(
        functools.partial(kernel, seq_count),
        out_shape=jax.ShapeDtypeStruct(queries.shape, bf16),
        in_specs=[hbm] * 5,
        out_specs=any_space,
        scratch_shapes=[
            pltpu.VMEM((BLOCK, WIDTH), bf16),
            pltpu.VMEM((2 * BLOCK, WIDTH), bf16),
            pltpu.VMEM((2 * BLOCK, WIDTH), bf16),
            pltpu.VMEM((BLOCK, WIDTH // 2), bf16),
            pltpu.VMEM((3 * BLOCK, WIDTH // 2), bf16),
            pltpu.VMEM((3 * BLOCK, WIDTH // 2), bf16),
            pltpu.VMEM((BLOCK, WIDTH // 2), bf16),
            pltpu.VMEM((HALF, 8, BLOCK), f32),
            pltpu.VMEM((BLOCK, WIDTH), bf16),
            pltpu.VMEM((CHUNKS, 8, BLOCK), f32),
            pltpu.VMEM((BLOCK, WIDTH), f32),
            pltpu.VMEM((HEADS, BLOCK, DIM), f32),
            pltpu.VMEM((HEADS, BLOCK, DIM), f32),
            pltpu.VMEM((BLOCK, WIDTH), bf16),
            pltpu.SMEM(alignment.shape[::-1], jnp.int32),
            pltpu.SMEM(cross_gate.shape, f32),
            block,
            block,
            block,
            block,
            pltpu.VMEM((CHUNKS, 8, BLOCK), f32),
            block,
            pltpu.VMEM((CHUNKS, 8, BLOCK), f32),
            block,
            block,
            dma((7,)),
            dma((CHUNKS,)),
            dma((2, CHUNKS)),
            dma((2, CHUNKS)),
            dma((2, CHUNKS)),
            dma((2, CHUNKS)),
            dma((2, CHUNKS)),
            dma((2, CHUNKS)),
            dma((HALF,)),
            dma((2,)),
            dma((2, HALF)),
            dma((CHUNKS,)),
            dma((CHUNKS,)),
            dma((3, CHUNKS)),
            dma((CHUNKS,)),
            dma((CHUNKS,)),
            dma((CHUNKS,)),
            dma((2, CHUNKS)),
        ],
        compiler_params=pltpu.CompilerParams(
            collective_id=0, has_side_effects=True, vmem_limit_bytes=52000000
        ),
    )(*(pltpu.with_memory_space_constraint(a, pltpu.HBM) for a in (jnp.transpose(alignment), cross_gate, queries, keys, values)))


def solution(mesh):
    placed = (P("tower", "seq", None), P("tower", "seq", None), P("tower", "seq", None), P(), P())
    return jax.shard_map(
        functools.partial(local, mesh.shape["seq"]),
        mesh=mesh,
        in_specs=placed,
        out_specs=P("tower", "seq", None),
        check_vma=False,
    )
```

```python
import functools
import math

import jax
import jax.numpy as jnp
from jax import lax
from jax.experimental import pallas as pl
from jax.experimental.pallas import tpu as pltpu
from jax.sharding import PartitionSpec as P

HEADS = 24
DIM = 128
BLOCK = 128
WIDTH = HEADS * DIM
PER = 2
CHUNKS = HEADS // PER
HALF = CHUNKS // 2
SPAN = PER * DIM
COLD = math.log2(math.e) / math.sqrt(DIM)
MESH = pl.DeviceIdType.MESH


def cols(chunk):
    return pl.ds(pl.multiple_of(chunk * SPAN, SPAN), SPAN)


def head_cols(head):
    return pl.ds(pl.multiple_of(head * DIM, DIM), DIM)


def loop(count, body):
    def step(i, carry):
        body(i)
        return carry

    lax.fori_loop(0, count, step, 0)


def mix(q, k, v, bias):
    scores = lax.dot_general(q, k, (((1,), (1,)), ((), ())), preferred_element_type=jnp.float32)
    if bias is not None:
        scores = scores + bias
    top = jnp.max(scores, axis=1, keepdims=True)
    weights = jnp.exp2((scores - top) * COLD)
    total = jnp.sum(weights, axis=1, keepdims=True)
    mixed = jnp.dot(weights.astype(jnp.bfloat16), v, preferred_element_type=jnp.float32)
    return mixed, top, total


def bias_row(linked, blocks):
    off = jnp.where(linked, 0.0, -jnp.inf).astype(jnp.float32)
    place = lax.broadcasted_iota(jnp.int32, (1, blocks * BLOCK), 1)
    return jnp.where(place >= (blocks - 1) * BLOCK, off, 0.0)


def kernel(
    seq_count,
    align_hbm,
    gate_hbm,
    q_hbm,
    k_hbm,
    v_hbm,
    out_hbm,
    q_own,
    main_k,
    main_v,
    aud_q,
    aud_k,
    aud_v,
    part_out,
    part_stat,
    part_in,
    stat_in,
    local_mix,
    local_top,
    local_total,
    out_buf,
    align_ref,
    gate_ref,
    edge_q,
    edge_out,
    edge_stat,
    edge_in,
    edge_stat_in,
    relay_k,
    relay_v,
    local_sem,
    out_sem,
    send_a,
    send_b,
    send_c,
    send_d,
    recv_near,
    recv_next,
    recv_q,
    recv_pair,
    recv_third,
    recv_part,
    recv_stat,
    send_e,
    recv_edge_q,
    recv_edge,
    recv_edge_stat,
    recv_relay,
):
    tower = lax.axis_index("tower")
    column = lax.axis_index("seq")
    is_first = column == 0
    is_last = column == seq_count - 1
    edge = seq_count // 2 - 1
    last = seq_count - 1
    at_edge = column == edge
    past_edge = column == edge + 1
    before = jnp.maximum(column - 1, 0)
    after = jnp.minimum(column + 1, seq_count - 1)
    sources = (k_hbm, v_hbm)
    mains = (main_k, main_v)
    auds = (aud_k, aud_v)

    def device(t, c):
        return {"tower": t, "seq": c}

    def remote(src, dst, send, recv, t, c):
        return pltpu.make_async_remote_copy(
            src_ref=src, dst_ref=dst, send_sem=send, recv_sem=recv, device_id=device(t, c), device_id_type=MESH
        )

    q_copy = pltpu.make_async_copy(q_hbm.at[0], q_own, local_sem.at[2])
    q_copy.start()
    small = (
        pltpu.make_async_copy(align_hbm, align_ref, local_sem.at[3]),
        pltpu.make_async_copy(gate_hbm, gate_ref, local_sem.at[4]),
    )
    for copy in small:
        copy.start()

    barrier = pltpu.get_barrier_semaphore()

    def greet(t, c):
        pl.semaphore_signal(barrier, inc=1, device_id=device(t, c), device_id_type=MESH)

    def meet(fixed, others):
        peers = jnp.int32(len(fixed))
        for t in fixed:
            greet(t, column)
        for when, t, c in others:

            @pl.when(when)
            def _():
                greet(t, c)

            peers = peers + jnp.where(when, 1, 0)
        pl.semaphore_wait(barrier, peers)

    has_back = jnp.logical_not(jnp.logical_or(is_first, past_edge))
    has_forward = jnp.logical_not(jnp.logical_or(is_last, at_edge))

    @pl.when(tower == 0)
    def _():
        meet(
            (1, 3),
            [
                (has_back, 0, before),
                (has_back, 1, before),
                (has_forward, 0, after),
                (past_edge, 2, edge),
                (past_edge, 3, edge),
                (is_last, 2, edge),
                (is_last, 3, edge + 1),
            ],
        )

    @pl.when(tower == 1)
    def _():
        meet((0, 3), [(has_forward, 0, after), (past_edge, 2, edge), (past_edge, 3, edge)])

    @pl.when(tower == 2)
    def _():
        meet((3,), [(has_forward, 3, after), (at_edge, 0, edge + 1), (at_edge, 1, edge + 1), (at_edge, 0, last)])

    @pl.when(tower == 3)
    def _():
        meet((0, 1, 2), [(has_back, 2, before), (at_edge, 0, edge + 1), (at_edge, 1, edge + 1), (past_edge, 0, last)])

    near_rows = pl.ds(0, BLOCK)
    next_rows = pl.ds(BLOCK, BLOCK)
    third_rows = pl.ds(2 * BLOCK, BLOCK)

    def await_own():
        q_copy.wait()
        for copy in small:
            copy.wait()

    def write_out(chunk):
        return pltpu.make_async_copy(
            out_buf.at[:, cols(chunk)], out_hbm.at[0, :, cols(chunk)], out_sem.at[chunk]
        )

    def recv_main(which, chunk, rows, sems):
        dst = mains[which].at[rows, cols(chunk)]
        return remote(dst, dst, send_a.at[which, chunk], sems.at[which, chunk], tower, column)

    def await_near(chunk):
        for which in range(2):
            recv_main(which, chunk, near_rows, recv_near).wait_recv()

    def await_next(chunk):
        for which in range(2):
            recv_main(which, chunk, next_rows, recv_next).wait_recv()

    def video_heads(chunk, blocks, bias):
        for i in range(PER):
            head = chunk * PER + i
            at = head_cols(head)
            mixed, _, total = mix(
                q_own[:, at], main_k[0 : blocks * BLOCK, at], main_v[0 : blocks * BLOCK, at], bias
            )
            out_buf[:, at] = (mixed * (gate_ref[0, head] / total)).astype(jnp.bfloat16)
        write_out(chunk).start()

    def finish_out(chunk):
        write_out(chunk).wait()

    @pl.when(tower < 2)
    def _():
        other = 1 - tower
        own_base = tower * HALF
        other_base = other * HALF
        own_rows = pl.ds(pl.multiple_of(tower * BLOCK, BLOCK), BLOCK)
        half_cols = pl.ds(pl.multiple_of(own_base * SPAN, SPAN), HALF * SPAN)
        other_cols = pl.ds(pl.multiple_of(other_base * SPAN, SPAN), HALF * SPAN)
        pair_rows = pl.ds(pl.multiple_of(other * BLOCK, BLOCK), BLOCK)

        def own_copy(which):
            return pltpu.make_async_copy(
                sources[which].at[0, :, half_cols], auds[which].at[own_rows, :], local_sem.at[which]
            )

        def pair_copy(which):
            return remote(
                sources[which].at[0, :, other_cols],
                auds[which].at[own_rows, :],
                send_c.at[which, 0],
                recv_pair.at[which],
                other,
                column,
            )

        def pair_wait(which):
            dst = auds[which].at[pair_rows, :]
            return remote(dst, dst, send_c.at[which, 0], recv_pair.at[which], tower, column)

        def third_copy(which, half, chunk):
            src = sources[which].at[0, :, cols(half * HALF + chunk)]
            dst = auds[which].at[third_rows, cols(chunk)]
            return remote(
                src, dst, send_d.at[which, half * HALF + chunk], recv_third.at[which, chunk], half, before
            )

        def third_wait(which, chunk):
            dst = auds[which].at[third_rows, cols(chunk)]
            return remote(dst, dst, send_d.at[which, chunk], recv_third.at[which, chunk], tower, column)

        def pass_pair(which, chunk):
            part = mains[which].at[near_rows, cols(chunk)]
            return remote(part, part, send_a.at[which, chunk], recv_near.at[which, chunk], other, column)

        def pass_next(which, chunk):
            return remote(
                mains[which].at[near_rows, cols(chunk)],
                mains[which].at[next_rows, cols(chunk)],
                send_b.at[which, chunk],
                recv_next.at[which, chunk],
                0,
                after,
            )

        def part_copy(chunk):
            return remote(
                part_out.at[:, cols(chunk)],
                part_in.at[:, cols(own_base + chunk)],
                send_c.at[0, 1 + chunk],
                recv_part.at[own_base + chunk],
                3,
                column,
            )

        def stat_copy(chunk):
            return remote(
                part_stat.at[chunk],
                stat_in.at[own_base + chunk],
                send_c.at[1, 1 + chunk],
                recv_stat.at[own_base + chunk],
                3,
                column,
            )

        def pass_back(which, chunk):
            return remote(
                mains[which].at[near_rows, cols(chunk)],
                mains[which].at[next_rows, cols(chunk)],
                send_d.at[which, chunk],
                recv_next.at[which, chunk],
                2,
                before,
            )

        lag = jnp.where(jnp.logical_and(tower == 0, past_edge), 2, 1)

        def edge_part(chunk):
            return remote(
                edge_out.at[:, cols(chunk)], edge_in.at[:, cols(chunk)], send_e.at[0, chunk], recv_edge.at[chunk], 3, edge
            )

        def edge_stats(chunk):
            return remote(
                edge_stat.at[chunk], edge_stat_in.at[chunk], send_e.at[1, chunk], recv_edge_stat.at[chunk], 3, edge
            )

        def pack(results):
            lane = lax.broadcasted_iota(jnp.int32, (BLOCK, DIM), 1)
            stat = jnp.zeros((BLOCK, DIM), jnp.float32)
            for i, (top, total) in enumerate(results):
                stat = jnp.where(lane == 2 * i, top, stat)
                stat = jnp.where(lane == 2 * i + 1, total, stat)
            return jnp.transpose(stat)[0:8]

        def attend_edge(step):
            chunk = own_base + step
            dst = edge_q.at[:, cols(chunk)]
            remote(dst, dst, send_e.at[0, chunk], recv_edge_q.at[chunk], tower, column).wait_recv()
            results = []
            for i in range(PER):
                at = head_cols(chunk * PER + i)
                key_at = head_cols(step * PER + i)
                mixed, top, total = mix(
                    edge_q[:, at], aud_k[0:BLOCK, key_at], aud_v[0:BLOCK, key_at], None
                )
                edge_out[:, at] = mixed.astype(jnp.bfloat16)
                results.append((top, total))
            edge_stat[chunk] = pack(results)
            edge_stats(chunk).start()
            edge_part(chunk).start()

        def relay_copy(which, chunk):
            return remote(
                (relay_k, relay_v)[which].at[:, cols(chunk)],
                mains[which].at[next_rows, cols(chunk)],
                send_e.at[which, chunk],
                recv_next.at[which, chunk],
                3,
                edge + 1,
            )

        def relay(chunk):
            for which in range(2):
                dst = (relay_k, relay_v)[which].at[:, cols(chunk)]
                remote(dst, dst, send_e.at[which, chunk], recv_relay.at[which, chunk], tower, column).wait_recv()
                relay_copy(which, chunk).start()

        for which in range(2):
            pair_copy(which).start()

        @pl.when(jnp.logical_and(tower == 0, has_back))
        def _():
            def start(chunk):
                for half in range(2):
                    for which in range(2):
                        third_copy(which, half, chunk).start()

            loop(HALF, start)

        for which in range(2):
            own_copy(which).start()

        @pl.when(jnp.logical_and(tower == 0, is_first))
        def _():
            for ref in mains:
                ref[BLOCK : 2 * BLOCK, :] = jnp.zeros((BLOCK, WIDTH), jnp.bfloat16)

        @pl.when(jnp.logical_not(has_forward))
        def _():
            for ref in auds:
                ref[2 * BLOCK : 3 * BLOCK, :] = jnp.zeros((BLOCK, WIDTH // 2), jnp.bfloat16)

        await_own()
        video_bias = bias_row(jnp.logical_and(column > 0, align_ref[1, before] > 3 * column), 2)
        audio_bias = bias_row(jnp.logical_and(has_forward, align_ref[1, column] > 3 * column + 3), 3)

        def video(step):
            @pl.when(tower == 0)
            def _():
                for base in (0, HALF):
                    chunk = base + step

                    @pl.when(jnp.logical_not(is_first))
                    def _():
                        await_next(chunk)

            await_near(other_base + step)

            @pl.when(tower == 0)
            def _():
                for base in (0, HALF):
                    video_heads(base + step, 2, video_bias)

            @pl.when(tower == 1)
            def _():
                for base in (0, HALF):
                    video_heads(base + step, 1, None)

        def take(step):
            chunk = own_base + step
            await_near(chunk)
            for which in range(2):
                pass_pair(which, chunk).start()

            @pl.when(has_forward)
            def _():
                for which in range(2):
                    pass_next(which, chunk).start()

            @pl.when(past_edge)
            def _():
                for which in range(2):
                    pass_back(which, chunk).start()

            @pl.when(jnp.logical_and(jnp.logical_and(tower == 0, is_last), jnp.logical_and(step > 0, step < 5)))
            def _():
                for i in range(3):
                    relay(3 * (step - 1) + i)

            @pl.when(jnp.logical_and(past_edge, step > 0))
            def _():
                attend_edge(step - 1)

            @pl.when(step >= lag)
            def _():
                video(step - lag)

            @pl.when(step > 0)
            def _():
                audio(step - 1)

        def audio(step):
            dst = aud_q.at[:, cols(step)]
            remote(dst, dst, send_a.at[0, step], recv_q.at[step], tower, column).wait_recv()

            @pl.when(has_forward)
            def _():
                for which in range(2):
                    third_wait(which, step).wait_recv()

            results = []
            for i in range(PER):
                at = head_cols(step * PER + i)
                mixed, top, total = mix(aud_q[:, at], aud_k[:, at], aud_v[:, at], audio_bias)
                part_out[:, at] = mixed.astype(jnp.bfloat16)
                results.append((top, total))
            part_stat[step] = pack(results)
            stat_copy(step).start()
            part_copy(step).start()

        for which in range(2):
            own_copy(which).wait()
            pair_wait(which).wait_recv()

        loop(HALF, take)

        @pl.when(past_edge)
        def _():
            attend_edge(HALF - 1)

        audio(HALF - 1)

        def rest(step, carry):
            video(step)
            return carry

        lax.fori_loop(HALF - lag, HALF, rest, 0)

        for which in range(2):
            pair_copy(which).wait_send()

        @pl.when(jnp.logical_and(tower == 0, has_back))
        def _():
            def drain(chunk):
                for half in range(2):
                    for which in range(2):
                        third_copy(which, half, chunk).wait_send()

            loop(HALF, drain)

        def drain(step):
            chunk = own_base + step
            for which in range(2):
                pass_pair(which, chunk).wait_send()

            @pl.when(has_forward)
            def _():
                for which in range(2):
                    pass_next(which, chunk).wait_send()

            @pl.when(past_edge)
            def _():
                for which in range(2):
                    pass_back(which, chunk).wait_send()

            stat_copy(step).wait_send()
            part_copy(step).wait_send()

        loop(HALF, drain)

        @pl.when(past_edge)
        def _():
            def drain_edge(step):
                edge_part(own_base + step).wait_send()
                edge_stats(own_base + step).wait_send()

            loop(HALF, drain_edge)

        @pl.when(jnp.logical_and(tower == 0, is_last))
        def _():
            def drain_relay(chunk):
                for which in range(2):
                    relay_copy(which, chunk).wait_send()

            loop(CHUNKS, drain_relay)

        loop(CHUNKS, finish_out)

    @pl.when(tower == 2)
    def _():
        def near_copy(which, chunk):
            return remote(
                sources[which].at[0, :, cols(chunk)],
                mains[which].at[near_rows, cols(chunk)],
                send_a.at[which, chunk],
                recv_near.at[which, chunk],
                3,
                column,
            )

        def next_copy(which, chunk):
            return remote(
                sources[which].at[0, :, cols(chunk)],
                mains[which].at[next_rows, cols(chunk)],
                send_b.at[which, chunk],
                recv_next.at[which, chunk],
                3,
                after,
            )

        def start_near(chunk):
            for which in range(2):
                near_copy(which, chunk).start()

        def start_next(chunk):
            for which in range(2):
                next_copy(which, chunk).start()

        def relay_in(which, chunk):
            return remote(
                sources[which].at[0, :, cols(chunk)],
                (relay_k, relay_v)[which].at[:, cols(chunk)],
                send_b.at[which, chunk],
                recv_relay.at[which, chunk],
                0,
                last,
            )

        @pl.when(has_forward)
        def _():
            loop(CHUNKS, start_next)

        @pl.when(at_edge)
        def _():
            def start_relay(chunk):
                for which in range(2):
                    relay_in(which, chunk).start()

            loop(CHUNKS, start_relay)

        loop(CHUNKS, start_near)

        @pl.when(is_last)
        def _():
            for ref in mains:
                ref[BLOCK : 2 * BLOCK, :] = jnp.zeros((BLOCK, WIDTH), jnp.bfloat16)

        await_own()
        linked = jnp.logical_and(column < seq_count - 1, align_ref[0, after] <= 3 * column + 2)
        bias = bias_row(linked, 2)

        def video(chunk):
            await_near(chunk)

            @pl.when(jnp.logical_not(is_last))
            def _():
                await_next(chunk)

            video_heads(chunk, 2, bias)

        loop(CHUNKS, video)

        def drain(chunk):
            for which in range(2):
                near_copy(which, chunk).wait_send()

            @pl.when(has_forward)
            def _():
                for which in range(2):
                    next_copy(which, chunk).wait_send()

            @pl.when(at_edge)
            def _():
                for which in range(2):
                    relay_in(which, chunk).wait_send()

            finish_out(chunk)

        loop(CHUNKS, drain)

    @pl.when(tower == 3)
    def _():
        def far_copy(which, half, step):
            chunk = half * HALF + step
            return remote(
                sources[which].at[0, :, cols(chunk)],
                mains[which].at[near_rows, cols(chunk)],
                send_a.at[which, chunk],
                recv_near.at[which, chunk],
                half,
                column,
            )

        def query_copy(half, step):
            return remote(
                q_hbm.at[0, :, cols(half * HALF + step)],
                aud_q.at[:, cols(step)],
                send_d.at[half, step],
                recv_q.at[step],
                half,
                column,
            )

        def near_copy(which, chunk):
            return remote(
                sources[which].at[0, :, cols(chunk)],
                mains[which].at[near_rows, cols(chunk)],
                send_b.at[which, chunk],
                recv_near.at[which, chunk],
                2,
                column,
            )

        def back_copy(which, chunk):
            return remote(
                sources[which].at[0, :, cols(chunk)],
                mains[which].at[next_rows, cols(chunk)],
                send_c.at[which, chunk],
                recv_next.at[which, chunk],
                2,
                before,
            )

        def edge_query(half, step):
            chunk = half * HALF + step
            return remote(
                q_hbm.at[0, :, cols(chunk)],
                edge_q.at[:, cols(chunk)],
                send_e.at[0, chunk],
                recv_edge_q.at[chunk],
                half,
                edge + 1,
            )

        def edge_copy(which, chunk):
            return remote(
                sources[which].at[0, :, cols(chunk)],
                mains[which].at[next_rows, cols(chunk)],
                send_e.at[1 + which, chunk],
                recv_next.at[which, chunk],
                0,
                edge + 1,
            )

        def start_far(step):
            for half in range(2):
                for which in range(2):
                    far_copy(which, half, step).start()

            @pl.when(step > 0)
            def _():
                for half in range(2):
                    query_copy(half, step - 1).start()

            @pl.when(jnp.logical_and(at_edge, step < HALF // 2))
            def _():
                for i in range(2):
                    for half in range(2):
                        edge_query(half, 2 * step + i).start()

            @pl.when(at_edge)
            def _():
                for half in range(2):
                    for which in range(2):
                        edge_copy(which, half * HALF + step).start()

        loop(HALF, start_far)
        for half in range(2):
            query_copy(half, HALF - 1).start()

        @pl.when(has_back)
        def _():
            def start_back(chunk):
                for which in range(2):
                    back_copy(which, chunk).start()

            loop(CHUNKS, start_back)

        def start_near(chunk):
            for which in range(2):
                near_copy(which, chunk).start()

        loop(CHUNKS, start_near)

        @pl.when(is_first)
        def _():
            for ref in mains:
                ref[BLOCK : 2 * BLOCK, :] = jnp.zeros((BLOCK, WIDTH), jnp.bfloat16)

        await_own()
        bias = bias_row(align_ref[0, column] <= 3 * column - 1, 2)

        def local(chunk):
            await_near(chunk)

            @pl.when(jnp.logical_not(is_first))
            def _():
                await_next(chunk)

            for i in range(PER):
                head = chunk * PER + i
                at = head_cols(head)
                mixed, top, total = mix(q_own[:, at], main_k[:, at], main_v[:, at], bias)
                local_mix[:, at] = mixed
                local_top[head] = jnp.broadcast_to(top, (BLOCK, DIM))
                local_total[head] = jnp.broadcast_to(total, (BLOCK, DIM))

        loop(CHUNKS, local)

        def unpack(rows):
            stat = jnp.concatenate([rows, jnp.zeros((DIM - 8, BLOCK), jnp.float32)], axis=0)
            return jnp.transpose(stat)

        @pl.when(at_edge)
        def _():
            reach = align_ref[1, column] > 3 * column + 3
            shift = jnp.where(reach, 0.0, -jnp.inf).astype(jnp.float32)

            def add_edge(chunk):
                dst = edge_stat_in.at[chunk]
                remote(dst, dst, send_a.at[0, chunk], recv_edge_stat.at[chunk], tower, column).wait_recv()
                dst = edge_in.at[:, cols(chunk)]
                remote(dst, dst, send_a.at[0, chunk], recv_edge.at[chunk], tower, column).wait_recv()
                stat = unpack(edge_stat_in[chunk])
                for i in range(PER):
                    head = chunk * PER + i
                    at = head_cols(head)
                    far_top = stat[:, 2 * i : 2 * i + 1] + shift
                    near_top = local_top[head][:, 0:1]
                    top = jnp.maximum(far_top, near_top)
                    far = jnp.exp2((far_top - top) * COLD)
                    near = jnp.exp2((near_top - top) * COLD)
                    total = far * stat[:, 2 * i + 1 : 2 * i + 2] + near * local_total[head][:, 0:1]
                    local_mix[:, at] = edge_in[:, at].astype(jnp.float32) * far + local_mix[:, at] * near
                    local_top[head] = jnp.broadcast_to(top, (BLOCK, DIM))
                    local_total[head] = jnp.broadcast_to(total, (BLOCK, DIM))

            def add_both(step):
                for half in range(2):
                    add_edge(half * HALF + step)

            loop(HALF, add_both)

        def merge_chunk(chunk):
            dst = stat_in.at[chunk]
            remote(dst, dst, send_a.at[0, chunk], recv_stat.at[chunk], tower, column).wait_recv()
            dst = part_in.at[:, cols(chunk)]
            remote(dst, dst, send_a.at[0, chunk], recv_part.at[chunk], tower, column).wait_recv()
            stat = unpack(stat_in[chunk])
            for i in range(PER):
                head = chunk * PER + i
                at = head_cols(head)
                far_top = stat[:, 2 * i : 2 * i + 1]
                far_total = stat[:, 2 * i + 1 : 2 * i + 2]
                near_top = local_top[head][:, 0:1]
                near_total = local_total[head][:, 0:1]
                top = jnp.maximum(far_top, near_top)
                far = jnp.exp2((far_top - top) * COLD)
                near = jnp.exp2((near_top - top) * COLD)
                scale = gate_ref[1, head] / (far * far_total + near * near_total)
                mixed = part_in[:, at].astype(jnp.float32) * (far * scale) + local_mix[:, at] * (near * scale)
                out_buf[:, at] = mixed.astype(jnp.bfloat16)
            write_out(chunk).start()

        def merge(step):
            for half in range(2):
                merge_chunk(half * HALF + step)

        loop(HALF, merge)

        def drain_far(step):
            for half in range(2):
                for which in range(2):
                    far_copy(which, half, step).wait_send()
                query_copy(half, step).wait_send()

            @pl.when(at_edge)
            def _():
                for half in range(2):
                    edge_query(half, step).wait_send()

        loop(HALF, drain_far)

        def drain(chunk):
            for which in range(2):
                near_copy(which, chunk).wait_send()

            @pl.when(has_back)
            def _():
                for which in range(2):
                    back_copy(which, chunk).wait_send()

            @pl.when(at_edge)
            def _():
                for which in range(2):
                    edge_copy(which, chunk).wait_send()

            finish_out(chunk)

        loop(CHUNKS, drain)


def local(seq_count, queries, keys, values, alignment, cross_gate):
    bf16, f32 = jnp.bfloat16, jnp.float32
    dma = pltpu.SemaphoreType.DMA
    any_space = pl.BlockSpec(memory_space=pl.ANY)
    block = pltpu.VMEM((BLOCK, WIDTH), bf16)
    hbm = pl.BlockSpec(memory_space=pltpu.HBM)
    return pl.pallas_call(
        functools.partial(kernel, seq_count),
        out_shape=jax.ShapeDtypeStruct(queries.shape, bf16),
        in_specs=[hbm] * 5,
        out_specs=any_space,
        scratch_shapes=[
            pltpu.VMEM((BLOCK, WIDTH), bf16),
            pltpu.VMEM((2 * BLOCK, WIDTH), bf16),
            pltpu.VMEM((2 * BLOCK, WIDTH), bf16),
            pltpu.VMEM((BLOCK, WIDTH // 2), bf16),
            pltpu.VMEM((3 * BLOCK, WIDTH // 2), bf16),
            pltpu.VMEM((3 * BLOCK, WIDTH // 2), bf16),
            pltpu.VMEM((BLOCK, WIDTH // 2), bf16),
            pltpu.VMEM((HALF, 8, BLOCK), f32),
            pltpu.VMEM((BLOCK, WIDTH), bf16),
            pltpu.VMEM((CHUNKS, 8, BLOCK), f32),
            pltpu.VMEM((BLOCK, WIDTH), f32),
            pltpu.VMEM((HEADS, BLOCK, DIM), f32),
            pltpu.VMEM((HEADS, BLOCK, DIM), f32),
            pltpu.VMEM((BLOCK, WIDTH), bf16),
            pltpu.SMEM(alignment.shape[::-1], jnp.int32),
            pltpu.SMEM(cross_gate.shape, f32),
            block,
            block,
            pltpu.VMEM((CHUNKS, 8, BLOCK), f32),
            block,
            pltpu.VMEM((CHUNKS, 8, BLOCK), f32),
            block,
            block,
            dma((5,)),
            dma((CHUNKS,)),
            dma((2, CHUNKS)),
            dma((2, CHUNKS)),
            dma((2, CHUNKS)),
            dma((2, CHUNKS)),
            dma((2, CHUNKS)),
            dma((2, CHUNKS)),
            dma((HALF,)),
            dma((2,)),
            dma((2, HALF)),
            dma((CHUNKS,)),
            dma((CHUNKS,)),
            dma((3, CHUNKS)),
            dma((CHUNKS,)),
            dma((CHUNKS,)),
            dma((CHUNKS,)),
            dma((2, CHUNKS)),
        ],
        compiler_params=pltpu.CompilerParams(
            collective_id=0, has_side_effects=True, vmem_limit_bytes=52000000
        ),
    )(*(pltpu.with_memory_space_constraint(a, pltpu.HBM) for a in (jnp.transpose(alignment), cross_gate, queries, keys, values)))


def solution(mesh):
    placed = (P("tower", "seq", None), P("tower", "seq", None), P("tower", "seq", None), P(), P())
    return jax.shard_map(
        functools.partial(local, mesh.shape["seq"]),
        mesh=mesh,
        in_specs=placed,
        out_specs=P("tower", "seq", None),
        check_vma=False,
    )
```

```python
import functools
import math

import jax
import jax.numpy as jnp
from jax import lax
from jax.experimental import pallas as pl
from jax.experimental.pallas import tpu as pltpu
from jax.sharding import PartitionSpec as P

HEADS = 24
DIM = 128
BLOCK = 128
WIDTH = HEADS * DIM
PER = 2
CHUNKS = HEADS // PER
HALF = CHUNKS // 2
SPAN = PER * DIM
COLD = math.log2(math.e) / math.sqrt(DIM)
MESH = pl.DeviceIdType.MESH


def cols(chunk):
    return pl.ds(pl.multiple_of(chunk * SPAN, SPAN), SPAN)


def head_cols(head):
    return pl.ds(pl.multiple_of(head * DIM, DIM), DIM)


def loop(count, body):
    def step(i, carry):
        body(i)
        return carry

    lax.fori_loop(0, count, step, 0)


def mix(q, k, v, bias):
    scores = lax.dot_general(q, k, (((1,), (1,)), ((), ())), preferred_element_type=jnp.float32)
    if bias is not None:
        scores = scores + bias
    top = jnp.max(scores, axis=1, keepdims=True)
    weights = jnp.exp2((scores - top) * COLD)
    total = jnp.sum(weights, axis=1, keepdims=True)
    mixed = jnp.dot(weights.astype(jnp.bfloat16), v, preferred_element_type=jnp.float32)
    return mixed, top, total


def bias_row(linked, blocks):
    off = jnp.where(linked, 0.0, -jnp.inf).astype(jnp.float32)
    place = lax.broadcasted_iota(jnp.int32, (1, blocks * BLOCK), 1)
    return jnp.where(place >= (blocks - 1) * BLOCK, off, 0.0)


def kernel(
    seq_count,
    align_hbm,
    gate_hbm,
    q_hbm,
    k_hbm,
    v_hbm,
    out_hbm,
    q_own,
    main_k,
    main_v,
    aud_q,
    aud_k,
    aud_v,
    part_out,
    part_stat,
    part_in,
    stat_in,
    local_mix,
    local_top,
    local_total,
    out_buf,
    align_ref,
    gate_ref,
    edge_q,
    edge_out,
    edge_stat,
    edge_in,
    edge_stat_in,
    relay_k,
    relay_v,
    local_sem,
    out_sem,
    send_a,
    send_b,
    send_c,
    send_d,
    recv_near,
    recv_next,
    recv_q,
    recv_pair,
    recv_third,
    recv_part,
    recv_stat,
    send_e,
    recv_edge_q,
    recv_edge,
    recv_edge_stat,
    recv_relay,
):
    tower = lax.axis_index("tower")
    column = lax.axis_index("seq")
    is_first = column == 0
    is_last = column == seq_count - 1
    edge = seq_count // 2 - 1
    last = seq_count - 1
    hub = seq_count - 4
    at_hub = column == hub
    at_edge = column == edge
    past_edge = column == edge + 1
    before = jnp.maximum(column - 1, 0)
    after = jnp.minimum(column + 1, seq_count - 1)
    sources = (k_hbm, v_hbm)
    mains = (main_k, main_v)
    auds = (aud_k, aud_v)

    def device(t, c):
        return {"tower": t, "seq": c}

    def remote(src, dst, send, recv, t, c):
        return pltpu.make_async_remote_copy(
            src_ref=src, dst_ref=dst, send_sem=send, recv_sem=recv, device_id=device(t, c), device_id_type=MESH
        )

    q_copy = pltpu.make_async_copy(q_hbm.at[0], q_own, local_sem.at[2])
    q_copy.start()
    small = (
        pltpu.make_async_copy(align_hbm, align_ref, local_sem.at[3]),
        pltpu.make_async_copy(gate_hbm, gate_ref, local_sem.at[4]),
    )
    for copy in small:
        copy.start()

    barrier = pltpu.get_barrier_semaphore()

    def greet(t, c):
        pl.semaphore_signal(barrier, inc=1, device_id=device(t, c), device_id_type=MESH)

    def meet(fixed, others):
        peers = jnp.int32(len(fixed))
        for t in fixed:
            greet(t, column)
        for when, t, c in others:

            @pl.when(when)
            def _():
                greet(t, c)

            peers = peers + jnp.where(when, 1, 0)
        pl.semaphore_wait(barrier, peers)

    has_back = jnp.logical_not(jnp.logical_or(is_first, past_edge))
    has_forward = jnp.logical_not(jnp.logical_or(is_last, at_edge))

    @pl.when(tower == 0)
    def _():
        meet(
            (1, 3),
            [
                (has_back, 0, before),
                (has_back, 1, before),
                (has_forward, 0, after),
                (past_edge, 0, hub),
                (past_edge, 3, edge),
                (at_hub, 0, edge + 1),
                (at_hub, 1, edge + 1),
                (at_hub, 2, edge),
                (is_last, 2, edge),
                (is_last, 3, edge + 1),
            ],
        )

    @pl.when(tower == 1)
    def _():
        meet((0, 3), [(has_forward, 0, after), (past_edge, 0, hub), (past_edge, 3, edge)])

    @pl.when(tower == 2)
    def _():
        meet((3,), [(has_forward, 3, after), (at_edge, 0, hub), (at_edge, 0, last)])

    @pl.when(tower == 3)
    def _():
        meet((0, 1, 2), [(has_back, 2, before), (at_edge, 0, edge + 1), (at_edge, 1, edge + 1), (past_edge, 0, last)])

    near_rows = pl.ds(0, BLOCK)
    next_rows = pl.ds(BLOCK, BLOCK)
    third_rows = pl.ds(2 * BLOCK, BLOCK)

    def await_own():
        q_copy.wait()
        for copy in small:
            copy.wait()

    def write_out(chunk):
        return pltpu.make_async_copy(
            out_buf.at[:, cols(chunk)], out_hbm.at[0, :, cols(chunk)], out_sem.at[chunk]
        )

    def recv_main(which, chunk, rows, sems):
        dst = mains[which].at[rows, cols(chunk)]
        return remote(dst, dst, send_a.at[which, chunk], sems.at[which, chunk], tower, column)

    def await_near(chunk):
        for which in range(2):
            recv_main(which, chunk, near_rows, recv_near).wait_recv()

    def await_next(chunk):
        for which in range(2):
            recv_main(which, chunk, next_rows, recv_next).wait_recv()

    def video_heads(chunk, blocks, bias):
        for i in range(PER):
            head = chunk * PER + i
            at = head_cols(head)
            mixed, _, total = mix(
                q_own[:, at], main_k[0 : blocks * BLOCK, at], main_v[0 : blocks * BLOCK, at], bias
            )
            out_buf[:, at] = (mixed * (gate_ref[0, head] / total)).astype(jnp.bfloat16)
        write_out(chunk).start()

    def finish_out(chunk):
        write_out(chunk).wait()

    @pl.when(tower < 2)
    def _():
        other = 1 - tower
        own_base = tower * HALF
        other_base = other * HALF
        own_rows = pl.ds(pl.multiple_of(tower * BLOCK, BLOCK), BLOCK)
        half_cols = pl.ds(pl.multiple_of(own_base * SPAN, SPAN), HALF * SPAN)
        other_cols = pl.ds(pl.multiple_of(other_base * SPAN, SPAN), HALF * SPAN)
        pair_rows = pl.ds(pl.multiple_of(other * BLOCK, BLOCK), BLOCK)

        def own_copy(which):
            return pltpu.make_async_copy(
                sources[which].at[0, :, half_cols], auds[which].at[own_rows, :], local_sem.at[which]
            )

        def pair_copy(which):
            return remote(
                sources[which].at[0, :, other_cols],
                auds[which].at[own_rows, :],
                send_c.at[which, 0],
                recv_pair.at[which],
                other,
                column,
            )

        def pair_wait(which):
            dst = auds[which].at[pair_rows, :]
            return remote(dst, dst, send_c.at[which, 0], recv_pair.at[which], tower, column)

        def third_copy(which, half, chunk):
            src = sources[which].at[0, :, cols(half * HALF + chunk)]
            dst = auds[which].at[third_rows, cols(chunk)]
            return remote(
                src, dst, send_d.at[which, half * HALF + chunk], recv_third.at[which, chunk], half, before
            )

        def third_wait(which, chunk):
            dst = auds[which].at[third_rows, cols(chunk)]
            return remote(dst, dst, send_d.at[which, chunk], recv_third.at[which, chunk], tower, column)

        def pass_pair(which, chunk):
            part = mains[which].at[near_rows, cols(chunk)]
            return remote(part, part, send_a.at[which, chunk], recv_near.at[which, chunk], other, column)

        def pass_next(which, chunk):
            return remote(
                mains[which].at[near_rows, cols(chunk)],
                mains[which].at[next_rows, cols(chunk)],
                send_b.at[which, chunk],
                recv_next.at[which, chunk],
                0,
                after,
            )

        def part_copy(chunk):
            return remote(
                part_out.at[:, cols(chunk)],
                part_in.at[:, cols(own_base + chunk)],
                send_c.at[0, 1 + chunk],
                recv_part.at[own_base + chunk],
                3,
                column,
            )

        def stat_copy(chunk):
            return remote(
                part_stat.at[chunk],
                stat_in.at[own_base + chunk],
                send_c.at[1, 1 + chunk],
                recv_stat.at[own_base + chunk],
                3,
                column,
            )

        def pass_back(which, chunk):
            return remote(
                mains[which].at[near_rows, cols(chunk)],
                (relay_k, relay_v)[which].at[:, cols(chunk)],
                send_d.at[which, chunk],
                recv_relay.at[which, chunk],
                0,
                hub,
            )

        lag = jnp.where(jnp.logical_and(tower == 0, past_edge), 2, 1)

        def edge_part(chunk):
            return remote(
                edge_out.at[:, cols(chunk)], edge_in.at[:, cols(chunk)], send_e.at[0, chunk], recv_edge.at[chunk], 3, edge
            )

        def edge_stats(chunk):
            return remote(
                edge_stat.at[chunk], edge_stat_in.at[chunk], send_e.at[1, chunk], recv_edge_stat.at[chunk], 3, edge
            )

        def pack(results):
            lane = lax.broadcasted_iota(jnp.int32, (BLOCK, DIM), 1)
            stat = jnp.zeros((BLOCK, DIM), jnp.float32)
            for i, (top, total) in enumerate(results):
                stat = jnp.where(lane == 2 * i, top, stat)
                stat = jnp.where(lane == 2 * i + 1, total, stat)
            return jnp.transpose(stat)[0:8]

        def attend_edge(step):
            chunk = own_base + step
            dst = edge_q.at[:, cols(chunk)]
            remote(dst, dst, send_e.at[0, chunk], recv_edge_q.at[chunk], tower, column).wait_recv()
            results = []
            for i in range(PER):
                at = head_cols(chunk * PER + i)
                key_at = head_cols(step * PER + i)
                mixed, top, total = mix(
                    edge_q[:, at], aud_k[0:BLOCK, key_at], aud_v[0:BLOCK, key_at], None
                )
                edge_out[:, at] = mixed.astype(jnp.bfloat16)
                results.append((top, total))
            edge_stat[chunk] = pack(results)
            edge_stats(chunk).start()
            edge_part(chunk).start()

        def relay_copy(which, chunk):
            return remote(
                (relay_k, relay_v)[which].at[:, cols(chunk)],
                mains[which].at[next_rows, cols(chunk)],
                send_e.at[which, chunk],
                recv_next.at[which, chunk],
                jnp.where(is_last, 3, 2),
                jnp.where(is_last, edge + 1, edge),
            )

        def relay(chunk):
            for which in range(2):
                dst = (relay_k, relay_v)[which].at[:, cols(chunk)]
                remote(dst, dst, send_e.at[which, chunk], recv_relay.at[which, chunk], tower, column).wait_recv()
                relay_copy(which, chunk).start()

        for which in range(2):
            pair_copy(which).start()

        @pl.when(jnp.logical_and(tower == 0, has_back))
        def _():
            def start(chunk):
                for half in range(2):
                    for which in range(2):
                        third_copy(which, half, chunk).start()

            loop(HALF, start)

        for which in range(2):
            own_copy(which).start()

        @pl.when(jnp.logical_and(tower == 0, is_first))
        def _():
            for ref in mains:
                ref[BLOCK : 2 * BLOCK, :] = jnp.zeros((BLOCK, WIDTH), jnp.bfloat16)

        @pl.when(jnp.logical_not(has_forward))
        def _():
            for ref in auds:
                ref[2 * BLOCK : 3 * BLOCK, :] = jnp.zeros((BLOCK, WIDTH // 2), jnp.bfloat16)

        await_own()
        video_bias = bias_row(jnp.logical_and(column > 0, align_ref[1, before] > 3 * column), 2)
        audio_bias = bias_row(jnp.logical_and(has_forward, align_ref[1, column] > 3 * column + 3), 3)

        def video(step):
            @pl.when(tower == 0)
            def _():
                for base in (0, HALF):
                    chunk = base + step

                    @pl.when(jnp.logical_not(is_first))
                    def _():
                        await_next(chunk)

            await_near(other_base + step)

            @pl.when(tower == 0)
            def _():
                for base in (0, HALF):
                    video_heads(base + step, 2, video_bias)

            @pl.when(tower == 1)
            def _():
                for base in (0, HALF):
                    video_heads(base + step, 1, None)

        def take(step):
            chunk = own_base + step
            await_near(chunk)
            for which in range(2):
                pass_pair(which, chunk).start()

            @pl.when(has_forward)
            def _():
                for which in range(2):
                    pass_next(which, chunk).start()

            @pl.when(past_edge)
            def _():
                for which in range(2):
                    pass_back(which, chunk).start()

            @pl.when(jnp.logical_and(jnp.logical_and(tower == 0, is_last), jnp.logical_and(step > 0, step < 5)))
            def _():
                for i in range(3):
                    relay(3 * (step - 1) + i)

            @pl.when(jnp.logical_and(jnp.logical_and(tower == 0, at_hub), step > 0))
            def _():
                for half in range(2):
                    relay(half * HALF + step - 1)

            @pl.when(jnp.logical_and(past_edge, step > 0))
            def _():
                attend_edge(step - 1)

            @pl.when(step >= lag)
            def _():
                video(step - lag)

            @pl.when(step > 0)
            def _():
                audio(step - 1)

        def audio(step):
            dst = aud_q.at[:, cols(step)]
            remote(dst, dst, send_a.at[0, step], recv_q.at[step], tower, column).wait_recv()

            @pl.when(has_forward)
            def _():
                for which in range(2):
                    third_wait(which, step).wait_recv()

            results = []
            for i in range(PER):
                at = head_cols(step * PER + i)
                mixed, top, total = mix(aud_q[:, at], aud_k[:, at], aud_v[:, at], audio_bias)
                part_out[:, at] = mixed.astype(jnp.bfloat16)
                results.append((top, total))
            part_stat[step] = pack(results)
            stat_copy(step).start()
            part_copy(step).start()

        for which in range(2):
            own_copy(which).wait()
            pair_wait(which).wait_recv()

        loop(HALF, take)

        @pl.when(jnp.logical_and(tower == 0, at_hub))
        def _():
            for half in range(2):
                relay(half * HALF + HALF - 1)

        @pl.when(past_edge)
        def _():
            attend_edge(HALF - 1)

        audio(HALF - 1)

        def rest(step, carry):
            video(step)
            return carry

        lax.fori_loop(HALF - lag, HALF, rest, 0)

        for which in range(2):
            pair_copy(which).wait_send()

        @pl.when(jnp.logical_and(tower == 0, has_back))
        def _():
            def drain(chunk):
                for half in range(2):
                    for which in range(2):
                        third_copy(which, half, chunk).wait_send()

            loop(HALF, drain)

        def drain(step):
            chunk = own_base + step
            for which in range(2):
                pass_pair(which, chunk).wait_send()

            @pl.when(has_forward)
            def _():
                for which in range(2):
                    pass_next(which, chunk).wait_send()

            @pl.when(past_edge)
            def _():
                for which in range(2):
                    pass_back(which, chunk).wait_send()

            stat_copy(step).wait_send()
            part_copy(step).wait_send()

        loop(HALF, drain)

        @pl.when(past_edge)
        def _():
            def drain_edge(step):
                edge_part(own_base + step).wait_send()
                edge_stats(own_base + step).wait_send()

            loop(HALF, drain_edge)

        @pl.when(jnp.logical_and(tower == 0, jnp.logical_or(is_last, at_hub)))
        def _():
            def drain_relay(chunk):
                for which in range(2):
                    relay_copy(which, chunk).wait_send()

            loop(CHUNKS, drain_relay)

        loop(CHUNKS, finish_out)

    @pl.when(tower == 2)
    def _():
        def near_copy(which, chunk):
            return remote(
                sources[which].at[0, :, cols(chunk)],
                mains[which].at[near_rows, cols(chunk)],
                send_a.at[which, chunk],
                recv_near.at[which, chunk],
                3,
                column,
            )

        def next_copy(which, chunk):
            return remote(
                sources[which].at[0, :, cols(chunk)],
                mains[which].at[next_rows, cols(chunk)],
                send_b.at[which, chunk],
                recv_next.at[which, chunk],
                3,
                after,
            )

        def start_near(chunk):
            for which in range(2):
                near_copy(which, chunk).start()

        def start_next(chunk):
            for which in range(2):
                next_copy(which, chunk).start()

        def relay_in(which, chunk):
            return remote(
                sources[which].at[0, :, cols(chunk)],
                (relay_k, relay_v)[which].at[:, cols(chunk)],
                send_b.at[which, chunk],
                recv_relay.at[which, chunk],
                0,
                last,
            )

        @pl.when(has_forward)
        def _():
            loop(CHUNKS, start_next)

        @pl.when(at_edge)
        def _():
            def start_relay(chunk):
                for which in range(2):
                    relay_in(which, chunk).start()

            loop(CHUNKS, start_relay)

        loop(CHUNKS, start_near)

        @pl.when(is_last)
        def _():
            for ref in mains:
                ref[BLOCK : 2 * BLOCK, :] = jnp.zeros((BLOCK, WIDTH), jnp.bfloat16)

        await_own()
        linked = jnp.logical_and(column < seq_count - 1, align_ref[0, after] <= 3 * column + 2)
        bias = bias_row(linked, 2)

        def video(chunk):
            await_near(chunk)

            @pl.when(jnp.logical_not(is_last))
            def _():
                await_next(chunk)

            video_heads(chunk, 2, bias)

        loop(CHUNKS, video)

        def drain(chunk):
            for which in range(2):
                near_copy(which, chunk).wait_send()

            @pl.when(has_forward)
            def _():
                for which in range(2):
                    next_copy(which, chunk).wait_send()

            @pl.when(at_edge)
            def _():
                for which in range(2):
                    relay_in(which, chunk).wait_send()

            finish_out(chunk)

        loop(CHUNKS, drain)

    @pl.when(tower == 3)
    def _():
        def far_copy(which, half, step):
            chunk = half * HALF + step
            return remote(
                sources[which].at[0, :, cols(chunk)],
                mains[which].at[near_rows, cols(chunk)],
                send_a.at[which, chunk],
                recv_near.at[which, chunk],
                half,
                column,
            )

        def query_copy(half, step):
            return remote(
                q_hbm.at[0, :, cols(half * HALF + step)],
                aud_q.at[:, cols(step)],
                send_d.at[half, step],
                recv_q.at[step],
                half,
                column,
            )

        def near_copy(which, chunk):
            return remote(
                sources[which].at[0, :, cols(chunk)],
                mains[which].at[near_rows, cols(chunk)],
                send_b.at[which, chunk],
                recv_near.at[which, chunk],
                2,
                column,
            )

        def back_copy(which, chunk):
            return remote(
                sources[which].at[0, :, cols(chunk)],
                mains[which].at[next_rows, cols(chunk)],
                send_c.at[which, chunk],
                recv_next.at[which, chunk],
                2,
                before,
            )

        def edge_query(half, step):
            chunk = half * HALF + step
            return remote(
                q_hbm.at[0, :, cols(chunk)],
                edge_q.at[:, cols(chunk)],
                send_e.at[0, chunk],
                recv_edge_q.at[chunk],
                half,
                edge + 1,
            )

        def edge_copy(which, chunk):
            return remote(
                sources[which].at[0, :, cols(chunk)],
                mains[which].at[next_rows, cols(chunk)],
                send_e.at[1 + which, chunk],
                recv_next.at[which, chunk],
                0,
                edge + 1,
            )

        def start_far(step):
            for half in range(2):
                for which in range(2):
                    far_copy(which, half, step).start()

            @pl.when(step > 0)
            def _():
                for half in range(2):
                    query_copy(half, step - 1).start()

            @pl.when(jnp.logical_and(at_edge, step < HALF // 2))
            def _():
                for i in range(2):
                    for half in range(2):
                        edge_query(half, 2 * step + i).start()

            @pl.when(at_edge)
            def _():
                for half in range(2):
                    for which in range(2):
                        edge_copy(which, half * HALF + step).start()

        loop(HALF, start_far)
        for half in range(2):
            query_copy(half, HALF - 1).start()

        @pl.when(has_back)
        def _():
            def start_back(chunk):
                for which in range(2):
                    back_copy(which, chunk).start()

            loop(CHUNKS, start_back)

        def start_near(chunk):
            for which in range(2):
                near_copy(which, chunk).start()

        loop(CHUNKS, start_near)

        @pl.when(is_first)
        def _():
            for ref in mains:
                ref[BLOCK : 2 * BLOCK, :] = jnp.zeros((BLOCK, WIDTH), jnp.bfloat16)

        await_own()
        bias = bias_row(align_ref[0, column] <= 3 * column - 1, 2)

        def local(chunk):
            await_near(chunk)

            @pl.when(jnp.logical_not(is_first))
            def _():
                await_next(chunk)

            for i in range(PER):
                head = chunk * PER + i
                at = head_cols(head)
                mixed, top, total = mix(q_own[:, at], main_k[:, at], main_v[:, at], bias)
                local_mix[:, at] = mixed
                local_top[head] = jnp.broadcast_to(top, (BLOCK, DIM))
                local_total[head] = jnp.broadcast_to(total, (BLOCK, DIM))

        loop(CHUNKS, local)

        def unpack(rows):
            stat = jnp.concatenate([rows, jnp.zeros((DIM - 8, BLOCK), jnp.float32)], axis=0)
            return jnp.transpose(stat)

        @pl.when(at_edge)
        def _():
            reach = align_ref[1, column] > 3 * column + 3
            shift = jnp.where(reach, 0.0, -jnp.inf).astype(jnp.float32)

            def add_edge(chunk):
                dst = edge_stat_in.at[chunk]
                remote(dst, dst, send_a.at[0, chunk], recv_edge_stat.at[chunk], tower, column).wait_recv()
                dst = edge_in.at[:, cols(chunk)]
                remote(dst, dst, send_a.at[0, chunk], recv_edge.at[chunk], tower, column).wait_recv()
                stat = unpack(edge_stat_in[chunk])
                for i in range(PER):
                    head = chunk * PER + i
                    at = head_cols(head)
                    far_top = stat[:, 2 * i : 2 * i + 1] + shift
                    near_top = local_top[head][:, 0:1]
                    top = jnp.maximum(far_top, near_top)
                    far = jnp.exp2((far_top - top) * COLD)
                    near = jnp.exp2((near_top - top) * COLD)
                    total = far * stat[:, 2 * i + 1 : 2 * i + 2] + near * local_total[head][:, 0:1]
                    local_mix[:, at] = edge_in[:, at].astype(jnp.float32) * far + local_mix[:, at] * near
                    local_top[head] = jnp.broadcast_to(top, (BLOCK, DIM))
                    local_total[head] = jnp.broadcast_to(total, (BLOCK, DIM))

            def add_both(step):
                for half in range(2):
                    add_edge(half * HALF + step)

            loop(HALF, add_both)

        def merge_chunk(chunk):
            dst = stat_in.at[chunk]
            remote(dst, dst, send_a.at[0, chunk], recv_stat.at[chunk], tower, column).wait_recv()
            dst = part_in.at[:, cols(chunk)]
            remote(dst, dst, send_a.at[0, chunk], recv_part.at[chunk], tower, column).wait_recv()
            stat = unpack(stat_in[chunk])
            for i in range(PER):
                head = chunk * PER + i
                at = head_cols(head)
                far_top = stat[:, 2 * i : 2 * i + 1]
                far_total = stat[:, 2 * i + 1 : 2 * i + 2]
                near_top = local_top[head][:, 0:1]
                near_total = local_total[head][:, 0:1]
                top = jnp.maximum(far_top, near_top)
                far = jnp.exp2((far_top - top) * COLD)
                near = jnp.exp2((near_top - top) * COLD)
                scale = gate_ref[1, head] / (far * far_total + near * near_total)
                mixed = part_in[:, at].astype(jnp.float32) * (far * scale) + local_mix[:, at] * (near * scale)
                out_buf[:, at] = mixed.astype(jnp.bfloat16)
            write_out(chunk).start()

        def merge(step):
            for half in range(2):
                merge_chunk(half * HALF + step)

        loop(HALF, merge)

        def drain_far(step):
            for half in range(2):
                for which in range(2):
                    far_copy(which, half, step).wait_send()
                query_copy(half, step).wait_send()

            @pl.when(at_edge)
            def _():
                for half in range(2):
                    edge_query(half, step).wait_send()

        loop(HALF, drain_far)

        def drain(chunk):
            for which in range(2):
                near_copy(which, chunk).wait_send()

            @pl.when(has_back)
            def _():
                for which in range(2):
                    back_copy(which, chunk).wait_send()

            @pl.when(at_edge)
            def _():
                for which in range(2):
                    edge_copy(which, chunk).wait_send()

            finish_out(chunk)

        loop(CHUNKS, drain)


def local(seq_count, queries, keys, values, alignment, cross_gate):
    bf16, f32 = jnp.bfloat16, jnp.float32
    dma = pltpu.SemaphoreType.DMA
    any_space = pl.BlockSpec(memory_space=pl.ANY)
    block = pltpu.VMEM((BLOCK, WIDTH), bf16)
    hbm = pl.BlockSpec(memory_space=pltpu.HBM)
    return pl.pallas_call(
        functools.partial(kernel, seq_count),
        out_shape=jax.ShapeDtypeStruct(queries.shape, bf16),
        in_specs=[hbm] * 5,
        out_specs=any_space,
        scratch_shapes=[
            pltpu.VMEM((BLOCK, WIDTH), bf16),
            pltpu.VMEM((2 * BLOCK, WIDTH), bf16),
            pltpu.VMEM((2 * BLOCK, WIDTH), bf16),
            pltpu.VMEM((BLOCK, WIDTH // 2), bf16),
            pltpu.VMEM((3 * BLOCK, WIDTH // 2), bf16),
            pltpu.VMEM((3 * BLOCK, WIDTH // 2), bf16),
            pltpu.VMEM((BLOCK, WIDTH // 2), bf16),
            pltpu.VMEM((HALF, 8, BLOCK), f32),
            pltpu.VMEM((BLOCK, WIDTH), bf16),
            pltpu.VMEM((CHUNKS, 8, BLOCK), f32),
            pltpu.VMEM((BLOCK, WIDTH), f32),
            pltpu.VMEM((HEADS, BLOCK, DIM), f32),
            pltpu.VMEM((HEADS, BLOCK, DIM), f32),
            pltpu.VMEM((BLOCK, WIDTH), bf16),
            pltpu.SMEM(alignment.shape[::-1], jnp.int32),
            pltpu.SMEM(cross_gate.shape, f32),
            block,
            block,
            pltpu.VMEM((CHUNKS, 8, BLOCK), f32),
            block,
            pltpu.VMEM((CHUNKS, 8, BLOCK), f32),
            block,
            block,
            dma((5,)),
            dma((CHUNKS,)),
            dma((2, CHUNKS)),
            dma((2, CHUNKS)),
            dma((2, CHUNKS)),
            dma((2, CHUNKS)),
            dma((2, CHUNKS)),
            dma((2, CHUNKS)),
            dma((HALF,)),
            dma((2,)),
            dma((2, HALF)),
            dma((CHUNKS,)),
            dma((CHUNKS,)),
            dma((3, CHUNKS)),
            dma((CHUNKS,)),
            dma((CHUNKS,)),
            dma((CHUNKS,)),
            dma((2, CHUNKS)),
        ],
        compiler_params=pltpu.CompilerParams(
            collective_id=0, has_side_effects=True, vmem_limit_bytes=52000000
        ),
    )(*(pltpu.with_memory_space_constraint(a, pltpu.HBM) for a in (jnp.transpose(alignment), cross_gate, queries, keys, values)))


def solution(mesh):
    placed = (P("tower", "seq", None), P("tower", "seq", None), P("tower", "seq", None), P(), P())
    return jax.shard_map(
        functools.partial(local, mesh.shape["seq"]),
        mesh=mesh,
        in_specs=placed,
        out_specs=P("tower", "seq", None),
        check_vma=False,
    )
```
